128 devices in a mesh: asc: 16 (over y, x), desc: 8 (over z, core).
Axes of the slice: x: 4, y: 4, z: 4, core: 2. Of those that a mesh axis runs over, the one named last changes fastest.
Arguments:
- coef_asc: float32 [4096, 128], P(('asc', 'desc')), may hold values from -0.3 to 0.3
- coef_desc: float32 [4096, 128], P(('asc', 'desc')), may hold values from -0.3 to 0.3
- cross_asc: int32 [8192, 128], P(('asc', 'desc')), may hold values from 0 to 4095, as said below
- cross_desc: int32 [8192, 128], P(('asc', 'desc')), may hold values from 0 to 4095, as said below
- time_asc: float32 [8192, 128], P(('asc', 'desc')), may hold values from 0 to 1
- time_desc: float32 [8192, 128], P(('asc', 'desc')), may hold values from 0 to 1
- height: float32 [8192, 128], P(('asc', 'desc')), may hold values from -18 to 18
- block_fill: int32 [8192], P(('asc', 'desc')), may hold values from 0 to 128, as said below
Outputs:
- adjusted_asc: float32 [4096, 128], P(('asc', 'desc'))
- adjusted_desc: float32 [4096, 128], P(('asc', 'desc'))
The draws below stay inside these ranges and needn't reach their ends.
Inputs may be any that keep to these rules, and one draw needn't show every extreme that they name: `cross_asc`: every crossover slot stored on a device of asc index p names an ascending arc a with a // 256 == p; slot s of every block names an arc a with (a // 32) % 8 == s % 8. `cross_desc`: every crossover slot stored on a device of desc index q names a descending arc d with (d // 32) % 8 == q; slot s of every block names an arc d with d // 256 == s % 16. `block_fill`: the slots in use stand first in each block; on each device the blocks with a nonzero count stand first and the first block is full; on some device all 64 blocks are in use.
All inputs are finite; a program needn't handle non-finite values.
Results may differ from the reference program's by a relative error of at most 0.0003.
Values sent between devices are 32-bit elements; how exact they have to be, the bound alone decides.
A program may use at most 64 MiB of HBM per device.

```python
import jax
import jax.numpy as jnp
from jax import lax

K = 128
BLOCK = 128
MAXB = 64
ARC_A_DEV = 32
ARC_D_DEV = 32
GN_STEPS = 2
CG_STEPS = 3
GROUP_A = 256
GROUP_D = 512
NA = 4096
ND = 4096
XROWS = 8192
N_ASC = 16
N_DESC = 8


def draw_cross_asc(key, part):
    row_device = jnp.arange(XROWS, dtype=jnp.int32) // MAXB
    desc_count = GROUP_A // ARC_A_DEV
    asc_group = row_device // desc_count
    column_owner = jnp.arange(BLOCK, dtype=jnp.int32) % desc_count
    within = jax.random.randint(jax.random.fold_in(key, 31), (XROWS, BLOCK), 0, ARC_A_DEV)
    return (asc_group[:, None] * GROUP_A + column_owner[None, :] * ARC_A_DEV + within).astype(jnp.int32)


def draw_cross_desc(key, part):
    row_device = jnp.arange(XROWS, dtype=jnp.int32) // MAXB
    desc_count = GROUP_A // ARC_A_DEV
    asc_count = GROUP_D // ARC_D_DEV
    desc_group = row_device % desc_count
    owner = (jnp.arange(BLOCK, dtype=jnp.int32) % asc_count)[None, :]
    within = jax.random.randint(jax.random.fold_in(key, 37), (XROWS, BLOCK), 0, ARC_D_DEV)
    return ((owner * desc_count + desc_group[:, None]) * ARC_D_DEV + within).astype(jnp.int32)


def draw_block_fill(key, part):
    device_count = XROWS // MAXB
    key_used, key_busy, key_fill = jax.random.split(jax.random.fold_in(key, 41), 3)
    used_blocks = jax.random.randint(key_used, (device_count,), MAXB // 4, MAXB // 2 + 1)
    busiest = jax.random.randint(key_busy, (), 0, device_count)
    used_blocks = jnp.where(jnp.arange(device_count) == busiest, MAXB, used_blocks)
    counts = jax.random.randint(key_fill, (device_count, MAXB), BLOCK // 2, BLOCK + 1)
    position = jnp.arange(MAXB)[None, :]
    counts = jnp.where(position == 0, BLOCK, counts)
    counts = jnp.where(position < used_blocks[:, None], counts, 0)
    return counts.reshape(-1).astype(jnp.int32)


def draw_height(key, part):
    key_scale, key_value = jax.random.split(jax.random.fold_in(key, 53))
    row_scale = jnp.exp(jax.random.uniform(key_scale, (XROWS, 1), minval=jnp.log(0.3), maxval=jnp.log(3.0)))
    base = jnp.clip(jax.random.normal(key_value, (XROWS, BLOCK)), -6.0, 6.0)
    return (row_scale * base).astype(jnp.float32)


def shard_levels(own_key, dims, shards, smallest, high):
    loudness, own = 1.0, jax.random.fold_in(own_key, 6)
    for dim, parts in shards:
        draws = jnp.exp(jax.random.uniform(jax.random.fold_in(own, dim), (parts,), jnp.float32, smallest / len(shards), high / len(shards)))
        loudness = loudness * jnp.repeat(draws, dims[dim] // parts).reshape([-1 if axis == dim else 1 for axis in range(len(dims))])
    return loudness


def scatter_about(key, shape, width, most, pieces=(), kind=jnp.bfloat16):
    gain = shard_levels(key, shape, pieces, -0.22, 0.18) if pieces else 1.0
    entries = jax.random.normal(key, shape, jnp.float32) * width * gain
    return jnp.minimum(jnp.maximum(entries, -most), most).astype(kind)


def setup_inputs(seed: int = 0) -> dict:
    streams_of = jax.random.split(jax.random.key(seed), 9)
    coef_asc = scatter_about(streams_of[0], (NA, K), 0.05, 0.3, ((0, 128),), jnp.float32)
    coef_desc = scatter_about(streams_of[1], (ND, K), 0.05, 0.3, ((0, 128),), jnp.float32)
    cross_asc = draw_cross_asc(jax.random.fold_in(streams_of[8], 71), 0)
    cross_desc = draw_cross_desc(jax.random.fold_in(streams_of[8], 71), 0)
    time_asc = jnp.clip(1.0 * jax.random.uniform(streams_of[4], (XROWS, BLOCK), jnp.float32) ** shard_levels(streams_of[4], (XROWS, BLOCK), ((0, 128),), -0.2, 0.2), 0.0, 1.0)
    time_desc = jnp.clip(1.0 * jax.random.uniform(streams_of[5], (XROWS, BLOCK), jnp.float32) ** shard_levels(streams_of[5], (XROWS, BLOCK), ((0, 128),), -0.2, 0.2), 0.0, 1.0)
    height = draw_height(jax.random.fold_in(streams_of[8], 71), 0)
    block_fill = draw_block_fill(jax.random.fold_in(streams_of[8], 71), 0)
    return dict(coef_asc=coef_asc, coef_desc=coef_desc, cross_asc=cross_asc, cross_desc=cross_desc, time_asc=time_asc, time_desc=time_desc, height=height, block_fill=block_fill)


damping = 2.0
cauchy_square = 2.25


def harmonics(times, term_count):
    half_terms = term_count // 2
    frequency = (lax.iota(jnp.int32, half_terms) + 1).astype(times.dtype)
    phases = jnp.pi * times[:, None] * frequency[None, :]
    return jnp.concatenate([jnp.cos(phases), jnp.sin(phases)], axis=1)


def device_rows(array, device):
    return lax.dynamic_slice_in_dim(array, (device * MAXB).astype(jnp.int32), MAXB, 0)


def crossover_pass(field_asc, field_desc, cross_asc, cross_desc, time_asc, time_desc, height, block_fill, weights, first_pass):
    def one_device(state_carry, device):
        grad_asc, grad_desc = state_carry
        ids_asc = device_rows(cross_asc, device).reshape(-1)
        ids_desc = device_rows(cross_desc, device).reshape(-1)
        basis_asc = harmonics(device_rows(time_asc, device).reshape(-1), K)
        basis_desc = harmonics(device_rows(time_desc, device).reshape(-1), K)
        block_counts = device_rows(block_fill, device)
        position = lax.broadcasted_iota(jnp.int32, (MAXB, BLOCK), 1)
        live_mask = (position < block_counts[:, None]).astype(field_asc.dtype).reshape(-1)
        modelled = jnp.sum(basis_asc * jnp.take(field_asc, ids_asc, axis=0), axis=1) - jnp.sum(
            basis_desc * jnp.take(field_desc, ids_desc, axis=0), axis=1)
        if first_pass:
            observed = device_rows(height, device).reshape(-1)
            misfit = live_mask * (observed - modelled)
            weight = live_mask / (1.0 + misfit * misfit / cauchy_square)
            weighted = weight * misfit
        else:
            weight = weights[device]
            weighted = weight * modelled
        grad_asc = grad_asc + jax.ops.segment_sum(weighted[:, None] * basis_asc, ids_asc, num_segments=NA)
        grad_desc = grad_desc - jax.ops.segment_sum(weighted[:, None] * basis_desc, ids_desc, num_segments=ND)
        return (grad_asc, grad_desc), weight

    start = (jnp.zeros((NA, K), field_asc.dtype), jnp.zeros((ND, K), field_asc.dtype))
    devices_all = jnp.arange(N_ASC * N_DESC, dtype=jnp.int32)
    (grad_asc, grad_desc), all_weights = lax.scan(one_device, start, devices_all)
    return grad_asc, grad_desc, all_weights


def pair_inner(first, second):
    return jnp.sum(first[0] * second[0]) + jnp.sum(first[1] * second[1])


def reference(coef_asc, coef_desc, cross_asc, cross_desc, time_asc, time_desc, height, block_fill):
    state_asc, state_desc = coef_asc, coef_desc
    for outer_step in range(GN_STEPS):
        grad_asc, grad_desc, weights = crossover_pass(state_asc, state_desc, cross_asc, cross_desc,
                                                      time_asc, time_desc, height, block_fill, None, True)
        remainder = (grad_asc - damping * state_asc, grad_desc - damping * state_desc)
        direction = remainder
        step_sum = (jnp.zeros_like(state_asc), jnp.zeros_like(state_desc))
        norm_now = pair_inner(remainder, remainder)
        for inner_step in range(CG_STEPS):
            part_asc, part_desc, unused = crossover_pass(direction[0], direction[1], cross_asc, cross_desc,
                                                         time_asc, time_desc, height, block_fill, weights, False)
            image_pair = (part_asc + damping * direction[0], part_desc + damping * direction[1])
            step_length = norm_now / pair_inner(direction, image_pair)
            step_sum = (step_sum[0] + step_length * direction[0], step_sum[1] + step_length * direction[1])
            if inner_step + 1 < CG_STEPS:
                remainder = (remainder[0] - step_length * image_pair[0], remainder[1] - step_length * image_pair[1])
                norm_next = pair_inner(remainder, remainder)
                ratio = norm_next / norm_now
                direction = (remainder[0] + ratio * direction[0], remainder[1] + ratio * direction[1])
                norm_now = norm_next
        state_asc = state_asc + step_sum[0]
        state_desc = state_desc + step_sum[1]
    return state_asc, state_desc
```

```python
import functools

import jax
import jax.numpy as jnp
import numpy as np
from jax import lax
from jax.experimental import pallas as pl
from jax.experimental.pallas import tpu as pltpu
from jax.sharding import PartitionSpec as P

MESH = pl.DeviceIdType.MESH
F32 = jnp.float32
BF16 = jnp.bfloat16
DAMPING = 2.0
INV_CAUCHY = 1.0 / 2.25
SLOTS = 16
HALF_PI_TERMS_SIN = [np.pi**n * s / f for n, s, f in ((1, 1, 1), (3, -1, 6), (5, 1, 120), (7, -1, 5040), (9, 1, 362880), (11, -1, 39916800))]
HALF_PI_TERMS_COS = [np.pi**n * s / f for n, s, f in ((0, 1, 1), (2, -1, 2), (4, 1, 24), (6, -1, 720), (8, 1, 40320), (10, -1, 3628800))]


def bits_of(p, q):
    y, x, z, c = p // 4, p % 4, q // 2, q % 2
    return (y // 2, x // 2, z // 2), (y % 2, x % 2, z % 2, c)


def cube_of(j):
    return (j % 2, (j // 2) % 2, j // 4)


def device_of(cube, member):
    return ((2 * cube[0] + member[0]) * 4 + 2 * cube[1] + member[1], (2 * cube[2] + member[2]) * 2 + member[3])


def asc_home(j, p):
    cube = cube_of(j)
    e = (p // 4 + 3 - 2 * cube[0] + 4) % 4
    f = (p % 4 + 3 - 2 * cube[1] + 4) % 4
    return cube, (e % 2, f % 2, e // 2, f // 2)


def asc_block(cube, member):
    y = (2 * cube[0] + member[0] + 1 + 2 * member[2]) % 4
    x = (2 * cube[1] + member[1] + 1 + 2 * member[3]) % 4
    return y * 4 + x


def desc_home(j, h, q):
    cube = cube_of(j)
    e = (q // 2 + 3 - 2 * cube[2] + 4) % 4
    return cube, ((h + cube[0] + cube[2]) % 2, e // 2, e % 2, q % 2)


def desc_block(cube, member):
    z = (2 * cube[2] + member[2] + 1 + 2 * member[1]) % 4
    h = (member[0] + cube[0] + cube[2]) % 2
    return h, z * 2 + member[3]


def slot_between(first, second):
    d = [(a + b) % 2 for a, b in zip(first, second)]
    return 8 * d[0] + 4 * d[1] + 2 * d[2] + d[3]


def partner(cube, member, r):
    d = (r // 8 % 2, r // 4 % 2, r // 2 % 2, r % 2)
    return device_of(cube, tuple((m + b) % 2 for m, b in zip(member, d)))


def turn(x):
    quarter = jnp.floor(2.0 * x + 0.5)
    f = x - 0.5 * quarter
    f2 = f * f
    s = jnp.full_like(f, HALF_PI_TERMS_SIN[-1])
    for term in HALF_PI_TERMS_SIN[-2::-1]:
        s = s * f2 + np.float32(term)
    s = s * f
    c = jnp.full_like(f, HALF_PI_TERMS_COS[-1])
    for term in HALF_PI_TERMS_COS[-2::-1]:
        c = c * f2 + np.float32(term)
    half = jnp.floor(0.5 * quarter)
    odd = quarter - 2.0 * half
    sign = 1.0 - 2.0 * (half - 2.0 * jnp.floor(0.5 * half))
    is_odd = odd > 0.5
    return sign * jnp.where(is_odd, -s, c), sign * jnp.where(is_odd, c, s)


def times(a, b):
    return a[0] * b[0] - a[1] * b[1], a[0] * b[1] + a[1] * b[0]


def split(value):
    high = value.astype(BF16)
    return high, (value - high.astype(F32)).astype(BF16)


def fold(value):
    return jnp.sum(value, axis=0, keepdims=True)


def kernel(
    coef_a, coef_d, ids_a, ids_d, time_a, time_d, height, fill,
    out_a, out_d,
    turned, stage_a, stage_d, got_a, got_d, coefs,
    basis_a, basis_d, mine_a, mine_d, theirs_a, theirs_d,
    weight_a, weight_d, err_a, err_d, y_a, y_d, vecs,
    part, ring_z, part_z, ring_xy, home_a, home_d,
    init_sem_a, init_sem_d, init_send, coef_sem, coef_send,
    swap_sem, swap_send, sum_sem, sum_send, home_sem, home_send,
):
    p, q = lax.axis_index("asc"), lax.axis_index("desc")
    cube, member = bits_of(p, q)
    me_class = 4 * cube[2] + 2 * cube[1] + cube[0]
    my_asc = asc_block(cube, member)
    my_h, my_q = desc_block(cube, member)
    my_i = me_class + 8 * my_h

    def at(cube_member):
        return device_of(*cube_member)

    barrier = pltpu.get_barrier_semaphore()

    def greet(device):
        pl.semaphore_signal(barrier, inc=1, device_id=device, device_id_type=MESH)

    def greet_column(k, carry):
        greet((my_asc, k))
        return carry

    def greet_row(k, carry):
        greet((k, my_q))
        return carry

    def greet_cube(k, carry):
        greet(partner(cube, member, k))
        return carry

    def greet_z(k, carry):
        greet((p, (q + k) % 8))
        return carry

    def greet_xy(k, carry):
        greet(((p + k) % 16, q))
        return carry

    lax.fori_loop(0, 8, greet_column, 0)
    lax.fori_loop(0, 16, greet_row, 0)
    lax.fori_loop(1, 16, greet_cube, 0)
    lax.fori_loop(1, 8, greet_z, 0)
    lax.fori_loop(1, 16, greet_xy, 0)
    greet(at(asc_home(q, p)))
    greet(at(desc_home(p % 8, p // 8, q)))

    row = lax.broadcasted_iota(jnp.int32, (64, 128), 0)
    lane = lax.broadcasted_iota(jnp.int32, (64, 128), 1)
    fill_row = fill[...].astype(F32)
    fills = jnp.concatenate([fill_row, fill_row], axis=1)
    slot = (row + 64 * (lane // 64)).astype(F32)
    live = slot < fills
    sources = (
        (ids_a[...] % 32).astype(F32),
        time_a[...],
        height[...],
        (ids_d[...] % 32).astype(F32),
        time_d[...],
    )
    for k, source in enumerate(sources):
        both = jnp.concatenate([source, pltpu.roll(source, 64, 1)], axis=0)
        flat = both.T[0:64]
        turned[k] = jnp.where(live, flat, -1.0) if k in (0, 3) else flat
    for i in range(16):
        for k in range(3):
            stage_a[i, k] = turned[k, pl.ds(i, 4, stride=16), :]
        for k in range(2):
            stage_d[i, k] = turned[3 + k, pl.ds(i, 4, stride=16), :]

    pl.semaphore_wait(barrier, 8 + 16 + 15 + 7 + 15 + 2)

    def coef_copy(side, source, device):
        return pltpu.make_async_remote_copy(
            src_ref=source, dst_ref=coefs.at[side], send_sem=coef_send.at[side], recv_sem=coef_sem.at[side],
            device_id=device, device_id_type=MESH,
        )

    send_coef_a = coef_copy(0, coef_a, at(asc_home(q, p)))
    send_coef_d = coef_copy(1, coef_d, at(desc_home(p % 8, p // 8, q)))
    send_coef_a.start()
    send_coef_d.start()

    def send_slots(i, carry):
        j, h = i % 8, i // 8
        a_home, d_home = asc_home(j, p), desc_home(j, h, q)
        r = slot_between(a_home[1], d_home[1])
        pltpu.make_async_remote_copy(
            src_ref=stage_a.at[i], dst_ref=got_a.at[r], send_sem=init_send.at[0], recv_sem=init_sem_a.at[r],
            device_id=at(a_home), device_id_type=MESH,
        ).start()
        pltpu.make_async_remote_copy(
            src_ref=stage_d.at[i], dst_ref=got_d.at[r], send_sem=init_send.at[1], recv_sem=init_sem_d.at[r],
            device_id=at(d_home), device_id_type=MESH,
        ).start()
        return carry

    lax.fori_loop(0, 16, send_slots, 0)

    frequency = (lax.broadcasted_iota(jnp.int32, (8, 128), 0) + 1).astype(F32)
    arc = lax.broadcasted_iota(jnp.int32, (32, 128), 0).astype(F32)

    def make_basis(r, got, basis):
        for l in range(4):
            t = jnp.broadcast_to(got[r, 1, l : l + 1, :], (8, 128))
            first = turn(frequency * t)
            e8 = tuple(jnp.broadcast_to(v[7:8], (8, 128)) for v in first)
            e16 = times(e8, e8)
            e32 = times(e16, e16)
            blocks = [first, times(first, e8)]
            blocks += [times(b, e16) for b in blocks]
            blocks += [times(b, e32) for b in blocks]
            terms = jnp.concatenate([b[0] for b in blocks] + [b[1] for b in blocks], axis=0)
            high, low = split(terms)
            basis[r, 0:128, 128 * l : 128 * (l + 1)] = high
            basis[r, 128:256, 128 * l : 128 * (l + 1)] = low

    def left_of(vector):
        high, low = split(vector)
        return jnp.concatenate(
            [jnp.concatenate([high, high], axis=1), jnp.concatenate([low, low], axis=1)], axis=0
        )

    def apply(r, left, got, basis, mine, par, take_height):
        terms = jnp.dot(left, basis[r], preferred_element_type=F32)
        terms = terms[0:32] + terms[32:64]
        for l in range(4):
            ids = jnp.broadcast_to(got[r, 0, l : l + 1, :], (32, 128))
            line = fold(jnp.where(ids == arc, terms[:, 128 * l : 128 * (l + 1)], 0.0))
            if take_height:
                line = line - got[r, 2, l : l + 1, :]
            mine[par, r, l : l + 1, :] = line

    def swap(par, r):
        device = partner(cube, member, r)
        return (
            pltpu.make_async_remote_copy(
                src_ref=mine_a.at[par, r], dst_ref=theirs_d.at[par, r],
                send_sem=swap_send.at[par, 0], recv_sem=swap_sem.at[par, 1, r],
                device_id=device, device_id_type=MESH,
            ),
            pltpu.make_async_remote_copy(
                src_ref=mine_d.at[par, r], dst_ref=theirs_a.at[par, r],
                send_sem=swap_send.at[par, 1], recv_sem=swap_sem.at[par, 0, r],
                device_id=device, device_id_type=MESH,
            ),
        )

    def forward(par, vector, build):
        left_a, left_d = left_of(vector[0:32]), left_of(vector[32:64])

        def one(r):
            if build:
                pltpu.make_async_copy(got_a.at[r], got_a.at[r], init_sem_a.at[r]).wait()
                pltpu.make_async_copy(got_d.at[r], got_d.at[r], init_sem_d.at[r]).wait()
                make_basis(r, got_a, basis_a)
                make_basis(r, got_d, basis_d)
            apply(r, left_a, got_a, basis_a, mine_a, par, build)
            apply(r, left_d, got_d, basis_d, mine_d, par, False)

        def step(k, carry):
            r = 15 - k
            one(r)
            for copy in swap(par, r):
                copy.start()
            return carry

        lax.fori_loop(0, 15, step, 0)
        one(0)
        theirs_a[par, 0] = mine_d[par, 0]
        theirs_d[par, 0] = mine_a[par, 0]

    def collect(par, r, z, got):
        high, low = split(z)
        lines = []
        for l in range(4):
            ids = jnp.broadcast_to(got[r, 0, l : l + 1, :], (32, 128))
            hit = ids == arc
            zs = jnp.broadcast_to(z[l : l + 1], (32, 128))
            zh, zl = split(jnp.where(hit, zs, 0.0))
            lines.append(jnp.concatenate([zh, zl], axis=0))
        return jnp.concatenate(lines, axis=1)

    def contract(placed, basis):
        return lax.dot_general(placed, basis, (((1,), (1,)), ((), ())), preferred_element_type=F32)

    def unfold(total):
        return total[0:32, 0:128] + (total[0:32, 128:256] + total[32:64, 0:128]) + total[32:64, 128:256]

    def backward(par, react):
        def one(r, carry):
            total_a, total_d = carry
            z_a, z_d = react(r)
            total_a += contract(collect(par, r, z_a, got_a), basis_a[r])
            total_d += contract(collect(par, r, z_d, got_d), basis_d[r])
            return total_a, total_d

        def step(r, carry):
            pltpu.make_async_copy(theirs_a.at[par, r], theirs_a.at[par, r], swap_sem.at[par, 0, r]).wait()
            pltpu.make_async_copy(theirs_d.at[par, r], theirs_d.at[par, r], swap_sem.at[par, 1, r]).wait()
            return one(r, carry)

        zero = jnp.zeros((64, 256), F32)
        total_a, total_d = lax.fori_loop(1, 16, step, one(0, (zero, zero)))
        wait_sent(par)
        return jnp.concatenate([unfold(total_a), unfold(total_d)], axis=0)

    def wait_sent(par):
        for k, mine in enumerate((mine_a, mine_d)):
            sent = mine.at[par, pl.ds(1, 15)]
            pltpu.make_async_copy(sent, sent, swap_send.at[par, k]).wait()

    def misfit(par, first):
        def react(r):
            if first:
                err_a[r] = mine_a[par, r] - theirs_a[par, r]
                err_d[r] = theirs_d[par, r] - mine_d[par, r]
            zs = []
            for err, got, weight in ((err_a, got_a, weight_a), (err_d, got_d, weight_d)):
                lives = jnp.where(got[r, 0] >= 0.0, 1.0, 0.0)
                m = -lives * err[r]
                w = lives / (1.0 + m * m * INV_CAUCHY)
                weight[r] = w
                zs.append(w * m)
            return zs[0], -zs[1]

        return react

    def image(par, n):
        def react(r):
            a = mine_a[par, r] - theirs_a[par, r]
            d = theirs_d[par, r] - mine_d[par, r]
            y_a[n, r] = a
            y_d[n, r] = d
            return weight_a[r] * a, -(weight_d[r] * d)

        return react

    def take(par, n):
        def step(r, carry):
            pltpu.make_async_copy(theirs_a.at[par, r], theirs_a.at[par, r], swap_sem.at[par, 0, r]).wait()
            pltpu.make_async_copy(theirs_d.at[par, r], theirs_d.at[par, r], swap_sem.at[par, 1, r]).wait()
            return carry

        lax.fori_loop(1, 16, step, 0)
        wait_sent(par)
        y_a[n] = mine_a[par] - theirs_a[par]
        y_d[n] = theirs_d[par] - mine_d[par]

    def sum_first(n, rows):
        rows = rows + [jnp.zeros((1, 128), F32)] * (8 - len(rows))
        part[n] = jnp.concatenate(rows, axis=0)

        def send(k, carry):
            pltpu.make_async_remote_copy(
                src_ref=part.at[n], dst_ref=ring_z.at[n, k], send_sem=sum_send.at[n, 0], recv_sem=sum_sem.at[n, 0],
                device_id=(p, (q + 8 - k) % 8), device_id_type=MESH,
            ).start()
            return carry

        lax.fori_loop(1, 8, send, 0)
        ring_z[n, 0] = part[n]

    def sum_second(n):
        whole = ring_z.at[n, pl.ds(1, 7)]
        pltpu.make_async_copy(whole, whole, sum_sem.at[n, 0]).wait()
        total = ring_z[n, (8 - q) % 8]
        for k in range(1, 8):
            total = total + ring_z[n, (k + 8 - q) % 8]
        part_z[n] = total

        def send(k, carry):
            pltpu.make_async_remote_copy(
                src_ref=part_z.at[n], dst_ref=ring_xy.at[n, k], send_sem=sum_send.at[n, 1], recv_sem=sum_sem.at[n, 1],
                device_id=((p + 16 - k) % 16, q), device_id_type=MESH,
            ).start()
            return carry

        lax.fori_loop(1, 16, send, 0)
        ring_xy[n, 0] = total

    def sum_last(n):
        whole = ring_xy.at[n, pl.ds(1, 15)]
        pltpu.make_async_copy(whole, whole, sum_sem.at[n, 1]).wait()
        total = ring_xy[n, (16 - p) % 16]
        for k in range(1, 16):
            total = total + ring_xy[n, (k + 16 - p) % 16]
        pltpu.make_async_copy(ring_z.at[n, pl.ds(1, 7)], ring_z.at[n, pl.ds(1, 7)], sum_send.at[n, 0]).wait()
        pltpu.make_async_copy(whole, whole, sum_send.at[n, 1]).wait()
        total = jnp.sum(total, axis=1, keepdims=True)
        return [total[k : k + 1, 0:1] for k in range(8)]

    def send_home(k):
        for side, buffer, device in ((0, home_a, (my_asc, me_class)), (1, home_d, (my_i, my_q))):
            pltpu.make_async_remote_copy(
                src_ref=vecs.at[k, pl.ds(32 * side, 32)], dst_ref=buffer.at[k],
                send_sem=home_send.at[side, k], recv_sem=home_sem.at[side, k],
                device_id=device, device_id_type=MESH,
            ).start()

    send_coef_a.wait_recv()
    send_coef_d.wait_recv()
    state = jnp.concatenate([coefs[0], coefs[1]], axis=0)
    par = 0
    forward(par, state, True)
    for step in range(2):
        last = step == 1
        if step == 0:
            gradient = backward(par, misfit(par, True))
            par = 1 - par
        else:
            react = misfit(par, False)

            def gather(r, carry):
                z_a, z_d = react(r)
                return (
                    carry[0] + contract(collect(0, r, z_a, got_a), basis_a[r]),
                    carry[1] + contract(collect(0, r, z_d, got_d), basis_d[r]),
                )

            zero = jnp.zeros((64, 256), F32)
            total_a, total_d = lax.fori_loop(0, 16, gather, (zero, zero))
            gradient = jnp.concatenate([unfold(total_a), unfold(total_d)], axis=0)
        r0 = gradient - DAMPING * state
        vecs[0] = state
        vecs[1] = r0
        forward(par, r0, False)
        if last:
            send_home(0)
            send_home(1)
        v1 = backward(par, image(par, 0)) + DAMPING * r0
        par = 1 - par
        vecs[2] = v1
        sum_first(2 * step, [fold(r0 * r0), fold(r0 * v1)])
        forward(par, v1, False)
        if last:
            send_home(2)
        sum_second(2 * step)
        v2 = backward(par, image(par, 1)) + DAMPING * v1
        par = 1 - par
        vecs[3] = v2
        forward(par, v2, False)
        if last:
            send_home(3)
        rr0, mu0 = sum_last(2 * step)[0:2]
        a0 = rr0 / mu0
        r1 = r0 - a0 * v1
        u1 = v1 - a0 * v2
        take(par, 2)
        par = 1 - par
        ju = y_a[1] - a0 * y_a[2]
        curve = jnp.sum(weight_a[...] * ju * ju, axis=0)
        sum_first(
            2 * step + 1,
            [fold(r1 * r1), fold(r1 * u1), fold(r1 * v1), fold(u1 * u1), fold(u1 * v1), fold(v1 * v1), fold(curve)],
        )
        sum_second(2 * step + 1)
        rr1, ru, rv, uu, uv, vv, wuu = sum_last(2 * step + 1)[0:7]
        b1 = rr1 / rr0
        a1 = rr1 / (ru + 2.0 * b1 * rv + b1 * b1 * mu0)
        g1 = a1 * b1
        rr2 = rr1 + a1 * a1 * uu + g1 * g1 * vv - 2.0 * a1 * ru - 2.0 * g1 * rv + 2.0 * a1 * g1 * uv
        rr2 = jnp.maximum(rr2, 0.0)
        b2 = rr2 / rr1
        pr, pu, pv, p0 = 1.0 + b2, -a1, -g1, b2 * b1
        m_uu, m_uv, m_vv = wuu + 2.0 * uu, (uv - uu) / a0, (vv - uv) / a0
        curve2 = (
            pr * pr * ru + pu * pu * m_uu + pv * pv * m_vv + p0 * p0 * mu0
            + 2.0 * (pr * pu * uu + pr * pv * uv + pr * p0 * rv + pu * pv * m_uv + pu * p0 * uv + pv * p0 * vv)
        )
        a2 = rr2 / jnp.maximum(curve2, jnp.maximum(2.0 * rr2, 1e-30))
        c_r = a1 + a2 * pr
        c_u = a2 * pu
        k0 = a0 + g1 + a2 * p0 + c_r
        k1 = a2 * pv - a0 * c_r + c_u
        k2 = -a0 * c_u
        if not last:
            state = state + (k0 * r0 + k1 * v1 + k2 * v2)
            for err, y in ((err_a, y_a), (err_d, y_d)):
                err[...] = err[...] + (k0 * y[0] + k1 * y[1] + k2 * y[2])

    send_coef_a.wait_send()
    send_coef_d.wait_send()
    pltpu.make_async_copy(stage_a, stage_a, init_send.at[0]).wait()
    pltpu.make_async_copy(stage_d, stage_d, init_send.at[1]).wait()
    for side, (buffer, out) in enumerate(((home_a, out_a), (home_d, out_d))):
        for k in range(4):
            pltpu.make_async_copy(buffer.at[k], buffer.at[k], home_sem.at[side, k]).wait()
            pltpu.make_async_copy(buffer.at[k], buffer.at[k], home_send.at[side, k]).wait()
        out[...] = buffer[0] + (k0 * buffer[1] + k1 * buffer[2] + k2 * buffer[3])


def body(coef_a, coef_d, cross_a, cross_d, time_a, time_d, height, fill):
    vmem = pl.BlockSpec(memory_space=pltpu.VMEM)
    values = pltpu.VMEM((SLOTS, 4, 128), F32)
    dma = pltpu.SemaphoreType.DMA
    return pl.pallas_call(
        kernel,
        out_shape=(jax.ShapeDtypeStruct((32, 128), F32),) * 2,
        in_specs=[vmem] * 8,
        out_specs=(vmem, vmem),
        scratch_shapes=[
            pltpu.VMEM((5, 64, 128), F32),
            pltpu.VMEM((16, 3, 4, 128), F32),
            pltpu.VMEM((16, 2, 4, 128), F32),
            pltpu.VMEM((SLOTS, 3, 4, 128), F32),
            pltpu.VMEM((SLOTS, 2, 4, 128), F32),
            pltpu.VMEM((2, 32, 128), F32),
            pltpu.VMEM((SLOTS, 256, 512), BF16),
            pltpu.VMEM((SLOTS, 256, 512), BF16),
            pltpu.VMEM((2, SLOTS, 4, 128), F32),
            pltpu.VMEM((2, SLOTS, 4, 128), F32),
            pltpu.VMEM((2, SLOTS, 4, 128), F32),
            pltpu.VMEM((2, SLOTS, 4, 128), F32),
            values,
            values,
            values,
            values,
            pltpu.VMEM((3, SLOTS, 4, 128), F32),
            pltpu.VMEM((3, SLOTS, 4, 128), F32),
            pltpu.VMEM((4, 64, 128), F32),
            pltpu.VMEM((4, 8, 128), F32),
            pltpu.VMEM((4, 8, 8, 128), F32),
            pltpu.VMEM((4, 8, 128), F32),
            pltpu.VMEM((4, 16, 8, 128), F32),
            pltpu.VMEM((4, 32, 128), F32),
            pltpu.VMEM((4, 32, 128), F32),
            dma((SLOTS,)),
            dma((SLOTS,)),
            dma((2,)),
            dma((2,)),
            dma((2,)),
            dma((2, 2, SLOTS)),
            dma((2, 2)),
            dma((4, 2)),
            dma((4, 2)),
            dma((2, 4)),
            dma((2, 4)),
        ],
        compiler_params=pltpu.CompilerParams(collective_id=0, has_side_effects=True),
        name="adjust",
    )(coef_a, coef_d, cross_a, cross_d, time_a, time_d, height, fill.reshape(1, -1))


def solution(mesh):
    rows = P(("asc", "desc"), None)
    return jax.shard_map(
        body,
        mesh=mesh,
        in_specs=(rows,) * 7 + (P(("asc", "desc")),),
        out_specs=(rows, rows),
        check_vma=False,
    )
```

```python
import functools

import jax
import jax.numpy as jnp
import numpy as np
from jax import lax
from jax.experimental import pallas as pl
from jax.experimental.pallas import tpu as pltpu
from jax.sharding import PartitionSpec as P

MESH = pl.DeviceIdType.MESH
F32 = jnp.float32
BF16 = jnp.bfloat16
DAMPING = 2.0
INV_CAUCHY = 1.0 / 2.25
SLOTS = 16
HALF_PI_TERMS_SIN = [np.pi**n * s / f for n, s, f in ((1, 1, 1), (3, -1, 6), (5, 1, 120), (7, -1, 5040), (9, 1, 362880), (11, -1, 39916800))]
HALF_PI_TERMS_COS = [np.pi**n * s / f for n, s, f in ((0, 1, 1), (2, -1, 2), (4, 1, 24), (6, -1, 720), (8, 1, 40320), (10, -1, 3628800))]


def div(a, n):
    return a // n if isinstance(a, int) else lax.div(a, jnp.int32(n))


def rem(a, n):
    return a % n if isinstance(a, int) else lax.rem(a, jnp.int32(n))


def bits_of(p, q):
    y, x, z, c = div(p, 4), rem(p, 4), div(q, 2), rem(q, 2)
    return (div(y, 2), div(x, 2), div(z, 2)), (rem(y, 2), rem(x, 2), rem(z, 2), c)


def cube_of(j):
    return (rem(j, 2), rem(div(j, 2), 2), div(j, 4))


def device_of(cube, member):
    return ((2 * cube[0] + member[0]) * 4 + 2 * cube[1] + member[1], (2 * cube[2] + member[2]) * 2 + member[3])


def asc_home(j, p):
    cube = cube_of(j)
    e = rem(div(p, 4) + 7 - 2 * cube[0], 4)
    f = rem(rem(p, 4) + 7 - 2 * cube[1], 4)
    return cube, (rem(e, 2), rem(f, 2), div(e, 2), div(f, 2))


def asc_block(cube, member):
    y = rem(2 * cube[0] + member[0] + 1 + 2 * member[2], 4)
    x = rem(2 * cube[1] + member[1] + 1 + 2 * member[3], 4)
    return y * 4 + x


def desc_home(j, h, q):
    cube = cube_of(j)
    e = rem(div(q, 2) + 7 - 2 * cube[2], 4)
    return cube, (rem(h + cube[0] + cube[2], 2), div(e, 2), rem(e, 2), rem(q, 2))


def desc_block(cube, member):
    z = rem(2 * cube[2] + member[2] + 1 + 2 * member[1], 4)
    h = rem(member[0] + cube[0] + cube[2], 2)
    return h, z * 2 + member[3]


def slot_between(first, second):
    d = [rem(a + b, 2) for a, b in zip(first, second)]
    return 8 * d[0] + 4 * d[1] + 2 * d[2] + d[3]


def partner(cube, member, high, low):
    d = (div(high, 2), rem(high, 2), div(low, 2), rem(low, 2))
    return device_of(cube, tuple(m if isinstance(b, int) and b == 0 else rem(m + b, 2) for m, b in zip(member, d)))


def turn(x):
    quarter = jnp.floor(2.0 * x + 0.5)
    f = x - 0.5 * quarter
    f2 = f * f
    s = jnp.full_like(f, HALF_PI_TERMS_SIN[-1])
    for term in HALF_PI_TERMS_SIN[-2::-1]:
        s = s * f2 + np.float32(term)
    s = s * f
    c = jnp.full_like(f, HALF_PI_TERMS_COS[-1])
    for term in HALF_PI_TERMS_COS[-2::-1]:
        c = c * f2 + np.float32(term)
    half = jnp.floor(0.5 * quarter)
    odd = quarter - 2.0 * half
    sign = 1.0 - 2.0 * (half - 2.0 * jnp.floor(0.5 * half))
    is_odd = odd > 0.5
    return sign * jnp.where(is_odd, -s, c), sign * jnp.where(is_odd, c, s)


def times(a, b):
    return a[0] * b[0] - a[1] * b[1], a[0] * b[1] + a[1] * b[0]


def split(value):
    high = value.astype(BF16)
    return high, (value - high.astype(F32)).astype(BF16)


def fold(value):
    return jnp.sum(value, axis=0, keepdims=True)


def kernel(
    coef_a, coef_d, ids_a, ids_d, time_a, time_d, height, fill,
    out_a, out_d,
    turned, stage_a, stage_d, got_a, got_d, coefs,
    basis_a, basis_d, mine_a, mine_d, theirs_a, theirs_d,
    weight_a, weight_d, err_a, err_d, y_a, y_d, vecs,
    part, ring_z, part_z, ring_xy, home_a, home_d,
    init_sem_a, init_sem_d, init_send, coef_sem, coef_send,
    swap_sem, swap_send, sum_sem, sum_send, home_sem, home_send,
):
    p, q = lax.axis_index("asc"), lax.axis_index("desc")
    cube, member = bits_of(p, q)
    me_class = 4 * cube[2] + 2 * cube[1] + cube[0]
    my_asc = asc_block(cube, member)
    my_h, my_q = desc_block(cube, member)
    my_i = me_class + 8 * my_h

    def at(cube_member):
        return device_of(*cube_member)

    barrier = pltpu.get_barrier_semaphore()

    def greet(device):
        pl.semaphore_signal(barrier, inc=1, device_id=device, device_id_type=MESH)

    for k in range(8):
        greet((my_asc, rem(q + k, 8)))
    for k in range(16):
        greet((rem(p + k, 16), my_q))
    for k in range(1, 16):
        greet(partner(cube, member, k // 4, k % 4))
    for k in range(1, 8):
        greet((p, rem(q + k, 8)))
    for k in range(1, 16):
        greet((rem(p + k, 16), q))
    greet(at(asc_home(q, p)))
    greet(at(desc_home(rem(p, 8), div(p, 8), q)))

    row = lax.broadcasted_iota(jnp.int32, (64, 128), 0)
    lane = lax.broadcasted_iota(jnp.int32, (64, 128), 1)
    fill_row = fill[...].astype(F32)
    fills = jnp.concatenate([fill_row, fill_row], axis=1)
    slot = (row + 64 * (lane // 64)).astype(F32)
    live = slot < fills
    sources = (
        (ids_a[...] % 32).astype(F32),
        time_a[...],
        height[...],
        (ids_d[...] % 32).astype(F32),
        time_d[...],
    )
    for k, source in enumerate(sources):
        both = jnp.concatenate([source, pltpu.roll(source, 64, 1)], axis=0)
        flat = both.T[0:64]
        turned[k] = jnp.where(live, flat, -1.0) if k in (0, 3) else flat
    for i in range(16):
        for k in range(3):
            stage_a[i, k] = turned[k, pl.ds(i, 4, stride=16), :]
        for k in range(2):
            stage_d[i, k] = turned[3 + k, pl.ds(i, 4, stride=16), :]

    pl.semaphore_wait(barrier, 8 + 16 + 15 + 7 + 15 + 2)

    def coef_copy(side, source, device):
        return pltpu.make_async_remote_copy(
            src_ref=source, dst_ref=coefs.at[side], send_sem=coef_send.at[side], recv_sem=coef_sem.at[side],
            device_id=device, device_id_type=MESH,
        )

    send_coef_a = coef_copy(0, coef_a, at(asc_home(q, p)))
    send_coef_d = coef_copy(1, coef_d, at(desc_home(rem(p, 8), div(p, 8), q)))
    send_coef_a.start()
    send_coef_d.start()

    def send_slots(k, carry):
        j = rem(k + q, 8)
        a_home = asc_home(j, p)
        for h in range(2):
            d_home = desc_home(j, h, q)
            r = slot_between(a_home[1], d_home[1])
            pltpu.make_async_remote_copy(
                src_ref=stage_a.at[j + 8 * h], dst_ref=got_a.at[r], send_sem=init_send.at[0], recv_sem=init_sem_a.at[r],
                device_id=at(a_home), device_id_type=MESH,
            ).start()
        j = rem(k + p, 8)
        a_home = asc_home(j, p)
        for h in range(2):
            d_home = desc_home(j, h, q)
            r = slot_between(a_home[1], d_home[1])
            pltpu.make_async_remote_copy(
                src_ref=stage_d.at[j + 8 * h], dst_ref=got_d.at[r], send_sem=init_send.at[1], recv_sem=init_sem_d.at[r],
                device_id=at(d_home), device_id_type=MESH,
            ).start()
        return carry

    lax.fori_loop(0, 8, send_slots, 0)

    frequency = (lax.broadcasted_iota(jnp.int32, (8, 128), 0) + 1).astype(F32)
    arc = lax.broadcasted_iota(jnp.int32, (32, 128), 0).astype(F32)

    def make_basis(r, got, basis):
        for l in range(4):
            t = jnp.broadcast_to(got[r, 1, l : l + 1, :], (8, 128))
            first = turn(frequency * t)
            e8 = tuple(jnp.broadcast_to(v[7:8], (8, 128)) for v in first)
            e16 = times(e8, e8)
            e32 = times(e16, e16)
            blocks = [first, times(first, e8)]
            blocks += [times(b, e16) for b in blocks]
            blocks += [times(b, e32) for b in blocks]
            terms = jnp.concatenate([b[0] for b in blocks] + [b[1] for b in blocks], axis=0)
            high, low = split(terms)
            basis[r, 0:128, 128 * l : 128 * (l + 1)] = high
            basis[r, 128:256, 128 * l : 128 * (l + 1)] = low

    def left_of(vector):
        high, low = split(vector)
        return jnp.concatenate(
            [jnp.concatenate([high, high], axis=1), jnp.concatenate([low, low], axis=1)], axis=0
        )

    def apply(r, left, got, basis, mine, par, take_height):
        terms = jnp.dot(left, basis[r], preferred_element_type=F32)
        terms = terms[0:32] + terms[32:64]
        for l in range(4):
            ids = jnp.broadcast_to(got[r, 0, l : l + 1, :], (32, 128))
            line = fold(jnp.where(ids == arc, terms[:, 128 * l : 128 * (l + 1)], 0.0))
            if take_height:
                line = line - got[r, 2, l : l + 1, :]
            mine[par, r, l : l + 1, :] = line

    def swap(par, high, low):
        device = partner(cube, member, high, low)
        r = 4 * high + low
        for mine, theirs, mine_kind in ((mine_a, theirs_d, 0), (mine_d, theirs_a, 1)):
            pltpu.make_async_remote_copy(
                src_ref=mine.at[par, r], dst_ref=theirs.at[par, r],
                send_sem=swap_send.at[par, mine_kind], recv_sem=swap_sem.at[par, 1 - mine_kind, r],
                device_id=device, device_id_type=MESH,
            ).start()

    def wait_swapped(par, r):
        for k, theirs in enumerate((theirs_a, theirs_d)):
            pltpu.make_async_copy(theirs.at[par, r], theirs.at[par, r], swap_sem.at[par, k, r]).wait()

    def forward(par, vector, build):
        left_a, left_d = left_of(vector[0:32]), left_of(vector[32:64])

        def prepare(r):
            pltpu.make_async_copy(got_a.at[r], got_a.at[r], init_sem_a.at[r]).wait()
            pltpu.make_async_copy(got_d.at[r], got_d.at[r], init_sem_d.at[r]).wait()
            make_basis(r, got_a, basis_a)
            make_basis(r, got_d, basis_d)

        def four(high):
            for low in range(3, -1, -1):
                r = 4 * high + low
                apply(r, left_a, got_a, basis_a, mine_a, par, build)
                apply(r, left_d, got_d, basis_d, mine_d, par, False)

        def step(k, carry):
            high = 3 - k
            if build:
                lax.fori_loop(4 * high, 4 * high + 4, lambda r, c: (prepare(r), c)[1], 0)
            four(high)
            for low in range(3, -1, -1):
                swap(par, high, low)
            return carry

        lax.fori_loop(0, 3, step, 0)
        if build:
            lax.fori_loop(0, 4, lambda r, c: (prepare(r), c)[1], 0)
        four(0)
        for low in range(3, 0, -1):
            swap(par, 0, low)
        theirs_a[par, 0] = mine_d[par, 0]
        theirs_d[par, 0] = mine_a[par, 0]

    def collect(par, r, z, got):
        high = z.astype(BF16).astype(F32)
        low = z - high
        lines = []
        for l in range(4):
            hit = jnp.broadcast_to(got[r, 0, l : l + 1, :], (32, 128)) == arc
            both = [jnp.where(hit, jnp.broadcast_to(v[l : l + 1], (32, 128)), 0.0) for v in (high, low)]
            lines.append(jnp.concatenate(both, axis=0).astype(BF16))
        return jnp.concatenate(lines, axis=1)

    def contract(placed, basis):
        return lax.dot_general(placed, basis, (((1,), (1,)), ((), ())), preferred_element_type=F32)

    def unfold(total):
        return total[0:32, 0:128] + (total[0:32, 128:256] + total[32:64, 0:128]) + total[32:64, 128:256]

    def backward(par, react, arriving=True):
        def four(high, carry, first):
            total_a, total_d = carry
            for low in range(4):
                r = 4 * high + low
                if arriving and not (first and low == 0):
                    wait_swapped(par, r)
                z_a, z_d = react(r)
                total_a += contract(collect(par, r, z_a, got_a), basis_a[r])
                total_d += contract(collect(par, r, z_d, got_d), basis_d[r])
            return total_a, total_d

        zero = jnp.zeros((64, 256), F32)
        total_a, total_d = lax.fori_loop(1, 4, lambda k, c: four(k, c, False), four(0, (zero, zero), True))
        if arriving:
            wait_sent(par)
        return jnp.concatenate([unfold(total_a), unfold(total_d)], axis=0)

    def wait_sent(par):
        for k, mine in enumerate((mine_a, mine_d)):
            sent = mine.at[par, pl.ds(1, 15)]
            pltpu.make_async_copy(sent, sent, swap_send.at[par, k]).wait()

    def misfit(par, first):
        def react(r):
            if first:
                err_a[r] = mine_a[par, r] - theirs_a[par, r]
                err_d[r] = theirs_d[par, r] - mine_d[par, r]
            zs = []
            for err, got, weight in ((err_a, got_a, weight_a), (err_d, got_d, weight_d)):
                lives = jnp.where(got[r, 0] >= 0.0, 1.0, 0.0)
                m = -lives * err[r]
                w = lives / (1.0 + m * m * INV_CAUCHY)
                weight[r] = w
                zs.append(w * m)
            return zs[0], -zs[1]

        return react

    def image(par, n):
        def react(r):
            a = mine_a[par, r] - theirs_a[par, r]
            d = theirs_d[par, r] - mine_d[par, r]
            y_a[n, r] = a
            y_d[n, r] = d
            return weight_a[r] * a, -(weight_d[r] * d)

        return react

    def take(par, n):
        lax.fori_loop(1, 16, lambda r, c: (wait_swapped(par, r), c)[1], 0)
        wait_sent(par)
        y_a[n] = mine_a[par] - theirs_a[par]
        y_d[n] = theirs_d[par] - mine_d[par]

    def sum_first(n, rows):
        rows = rows + [jnp.zeros((1, 128), F32)] * (8 - len(rows))
        part[n] = jnp.concatenate(rows, axis=0)

        def send(k, carry):
            pltpu.make_async_remote_copy(
                src_ref=part.at[n], dst_ref=ring_z.at[n, k], send_sem=sum_send.at[n, 0], recv_sem=sum_sem.at[n, 0],
                device_id=(p, rem(q + 8 - k, 8)), device_id_type=MESH,
            ).start()
            return carry

        lax.fori_loop(1, 8, send, 0)
        ring_z[n, 0] = part[n]

    def sum_second(n):
        whole = ring_z.at[n, pl.ds(1, 7)]
        pltpu.make_async_copy(whole, whole, sum_sem.at[n, 0]).wait()
        total = ring_z[n, rem(8 - q, 8)]
        for k in range(1, 8):
            total = total + ring_z[n, rem(k + 8 - q, 8)]
        part_z[n] = total

        def send(k, carry):
            pltpu.make_async_remote_copy(
                src_ref=part_z.at[n], dst_ref=ring_xy.at[n, k], send_sem=sum_send.at[n, 1], recv_sem=sum_sem.at[n, 1],
                device_id=(rem(p + 16 - k, 16), q), device_id_type=MESH,
            ).start()
            return carry

        lax.fori_loop(1, 16, send, 0)
        ring_xy[n, 0] = total

    def sum_last(n):
        whole = ring_xy.at[n, pl.ds(1, 15)]
        pltpu.make_async_copy(whole, whole, sum_sem.at[n, 1]).wait()
        total = ring_xy[n, rem(16 - p, 16)]
        for k in range(1, 16):
            total = total + ring_xy[n, rem(k + 16 - p, 16)]
        pltpu.make_async_copy(ring_z.at[n, pl.ds(1, 7)], ring_z.at[n, pl.ds(1, 7)], sum_send.at[n, 0]).wait()
        pltpu.make_async_copy(whole, whole, sum_send.at[n, 1]).wait()
        total = jnp.sum(total, axis=1, keepdims=True)
        return [total[k : k + 1, 0:1] for k in range(8)]

    def send_home(k):
        for side, buffer, device in ((0, home_a, (my_asc, me_class)), (1, home_d, (my_i, my_q))):
            pltpu.make_async_remote_copy(
                src_ref=vecs.at[k, pl.ds(32 * side, 32)], dst_ref=buffer.at[k],
                send_sem=home_send.at[side, k], recv_sem=home_sem.at[side, k],
                device_id=device, device_id_type=MESH,
            ).start()

    send_coef_a.wait_recv()
    send_coef_d.wait_recv()
    state = jnp.concatenate([coefs[0], coefs[1]], axis=0)
    par = 0
    forward(par, state, True)
    for step in range(2):
        last = step == 1
        if step == 0:
            gradient = backward(par, misfit(par, True))
            par = 1 - par
        else:
            gradient = backward(par, misfit(par, False), arriving=False)
        r0 = gradient - DAMPING * state
        vecs[0] = state
        vecs[1] = r0
        forward(par, r0, False)
        if last:
            send_home(0)
            send_home(1)
        v1 = backward(par, image(par, 0)) + DAMPING * r0
        par = 1 - par
        vecs[2] = v1
        sum_first(2 * step, [fold(r0 * r0), fold(r0 * v1)])
        forward(par, v1, False)
        if last:
            send_home(2)
        sum_second(2 * step)
        v2 = backward(par, image(par, 1)) + DAMPING * v1
        par = 1 - par
        vecs[3] = v2
        forward(par, v2, False)
        if last:
            send_home(3)
        rr0, mu0 = sum_last(2 * step)[0:2]
        a0 = rr0 / mu0
        r1 = r0 - a0 * v1
        u1 = v1 - a0 * v2
        take(par, 2)
        par = 1 - par
        ju = y_a[1] - a0 * y_a[2]
        curve = jnp.sum(weight_a[...] * ju * ju, axis=0)
        sum_first(
            2 * step + 1,
            [fold(r1 * r1), fold(r1 * u1), fold(r1 * v1), fold(u1 * u1), fold(u1 * v1), fold(v1 * v1), fold(curve)],
        )
        sum_second(2 * step + 1)
        rr1, ru, rv, uu, uv, vv, wuu = sum_last(2 * step + 1)[0:7]
        b1 = rr1 / rr0
        a1 = rr1 / (ru + 2.0 * b1 * rv + b1 * b1 * mu0)
        g1 = a1 * b1
        rr2 = rr1 + a1 * a1 * uu + g1 * g1 * vv - 2.0 * a1 * ru - 2.0 * g1 * rv + 2.0 * a1 * g1 * uv
        rr2 = jnp.maximum(rr2, 0.0)
        b2 = rr2 / rr1
        pr, pu, pv, p0 = 1.0 + b2, -a1, -g1, b2 * b1
        m_uu, m_uv, m_vv = wuu + 2.0 * uu, (uv - uu) / a0, (vv - uv) / a0
        curve2 = (
            pr * pr * ru + pu * pu * m_uu + pv * pv * m_vv + p0 * p0 * mu0
            + 2.0 * (pr * pu * uu + pr * pv * uv + pr * p0 * rv + pu * pv * m_uv + pu * p0 * uv + pv * p0 * vv)
        )
        a2 = rr2 / jnp.maximum(curve2, jnp.maximum(2.0 * rr2, 1e-30))
        c_r = a1 + a2 * pr
        c_u = a2 * pu
        k0 = a0 + g1 + a2 * p0 + c_r
        k1 = a2 * pv - a0 * c_r + c_u
        k2 = -a0 * c_u
        if not last:
            state = state + (k0 * r0 + k1 * v1 + k2 * v2)
            for err, y in ((err_a, y_a), (err_d, y_d)):
                err[...] = err[...] + (k0 * y[0] + k1 * y[1] + k2 * y[2])

    send_coef_a.wait_send()
    send_coef_d.wait_send()
    pltpu.make_async_copy(stage_a, stage_a, init_send.at[0]).wait()
    pltpu.make_async_copy(stage_d, stage_d, init_send.at[1]).wait()
    for side, (buffer, out) in enumerate(((home_a, out_a), (home_d, out_d))):
        for k in range(4):
            pltpu.make_async_copy(buffer.at[k], buffer.at[k], home_sem.at[side, k]).wait()
            pltpu.make_async_copy(buffer.at[k], buffer.at[k], home_send.at[side, k]).wait()
        out[...] = buffer[0] + (k0 * buffer[1] + k1 * buffer[2] + k2 * buffer[3])


def body(coef_a, coef_d, cross_a, cross_d, time_a, time_d, height, fill):
    vmem = pl.BlockSpec(memory_space=pltpu.VMEM)
    values = pltpu.VMEM((SLOTS, 4, 128), F32)
    dma = pltpu.SemaphoreType.DMA
    return pl.pallas_call(
        kernel,
        out_shape=(jax.ShapeDtypeStruct((32, 128), F32),) * 2,
        in_specs=[vmem] * 8,
        out_specs=(vmem, vmem),
        scratch_shapes=[
            pltpu.VMEM((5, 64, 128), F32),
            pltpu.VMEM((16, 3, 4, 128), F32),
            pltpu.VMEM((16, 2, 4, 128), F32),
            pltpu.VMEM((SLOTS, 3, 4, 128), F32),
            pltpu.VMEM((SLOTS, 2, 4, 128), F32),
            pltpu.VMEM((2, 32, 128), F32),
            pltpu.VMEM((SLOTS, 256, 512), BF16),
            pltpu.VMEM((SLOTS, 256, 512), BF16),
            pltpu.VMEM((2, SLOTS, 4, 128), F32),
            pltpu.VMEM((2, SLOTS, 4, 128), F32),
            pltpu.VMEM((2, SLOTS, 4, 128), F32),
            pltpu.VMEM((2, SLOTS, 4, 128), F32),
            values,
            values,
            values,
            values,
            pltpu.VMEM((3, SLOTS, 4, 128), F32),
            pltpu.VMEM((3, SLOTS, 4, 128), F32),
            pltpu.VMEM((4, 64, 128), F32),
            pltpu.VMEM((4, 8, 128), F32),
            pltpu.VMEM((4, 8, 8, 128), F32),
            pltpu.VMEM((4, 8, 128), F32),
            pltpu.VMEM((4, 16, 8, 128), F32),
            pltpu.VMEM((4, 32, 128), F32),
            pltpu.VMEM((4, 32, 128), F32),
            dma((SLOTS,)),
            dma((SLOTS,)),
            dma((2,)),
            dma((2,)),
            dma((2,)),
            dma((2, 2, SLOTS)),
            dma((2, 2)),
            dma((4, 2)),
            dma((4, 2)),
            dma((2, 4)),
            dma((2, 4)),
        ],
        compiler_params=pltpu.CompilerParams(collective_id=0, has_side_effects=True),
        name="adjust",
    )(coef_a, coef_d, cross_a, cross_d, time_a, time_d, height, fill.reshape(1, -1))


def solution(mesh):
    rows = P(("asc", "desc"), None)
    return jax.shard_map(
        body,
        mesh=mesh,
        in_specs=(rows,) * 7 + (P(("asc", "desc")),),
        out_specs=(rows, rows),
        check_vma=False,
    )
```

```python
import functools

import jax
import jax.numpy as jnp
import numpy as np
from jax import lax
from jax.experimental import pallas as pl
from jax.experimental.pallas import tpu as pltpu
from jax.sharding import PartitionSpec as P

MESH = pl.DeviceIdType.MESH
F32 = jnp.float32
BF16 = jnp.bfloat16
DAMPING = 2.0
INV_CAUCHY = 1.0 / 2.25
SLOTS = 16
HALF_PI_TERMS_SIN = [np.pi**n * s / f for n, s, f in ((1, 1, 1), (3, -1, 6), (5, 1, 120), (7, -1, 5040), (9, 1, 362880), (11, -1, 39916800))]
HALF_PI_TERMS_COS = [np.pi**n * s / f for n, s, f in ((0, 1, 1), (2, -1, 2), (4, 1, 24), (6, -1, 720), (8, 1, 40320), (10, -1, 3628800))]


def div(a, n):
    return a // n if isinstance(a, int) else lax.div(a, jnp.int32(n))


def rem(a, n):
    return a % n if isinstance(a, int) else lax.rem(a, jnp.int32(n))


def bits_of(p, q):
    y, x, z, c = div(p, 4), rem(p, 4), div(q, 2), rem(q, 2)
    return (div(y, 2), div(x, 2), div(z, 2)), (rem(y, 2), rem(x, 2), rem(z, 2), c)


def cube_of(j):
    return (rem(j, 2), rem(div(j, 2), 2), div(j, 4))


def device_of(cube, member):
    return ((2 * cube[0] + member[0]) * 4 + 2 * cube[1] + member[1], (2 * cube[2] + member[2]) * 2 + member[3])


def asc_home(j, p):
    cube = cube_of(j)
    e = rem(div(p, 4) + 7 - 2 * cube[0], 4)
    f = rem(rem(p, 4) + 7 - 2 * cube[1], 4)
    return cube, (rem(e, 2), rem(f, 2), div(e, 2), div(f, 2))


def asc_block(cube, member):
    y = rem(2 * cube[0] + member[0] + 1 + 2 * member[2], 4)
    x = rem(2 * cube[1] + member[1] + 1 + 2 * member[3], 4)
    return y * 4 + x


def desc_home(j, h, q):
    cube = cube_of(j)
    e = rem(div(q, 2) + 7 - 2 * cube[2], 4)
    return cube, (rem(h + cube[0] + cube[2], 2), div(e, 2), rem(e, 2), rem(q, 2))


def desc_block(cube, member):
    z = rem(2 * cube[2] + member[2] + 1 + 2 * member[1], 4)
    h = rem(member[0] + cube[0] + cube[2], 2)
    return h, z * 2 + member[3]


def slot_between(first, second):
    dy, dx, dz, dc = [rem(a + b, 2) for a, b in zip(first, second)]
    mid = rem(dy + dx, 2)
    group = mid * (1 + dz) + (1 - mid) * 3 * dy
    return 4 * group + 2 * (mid * dy + (1 - mid) * dz) + dc


def partner(cube, member, group, low):
    upper, core = low // 2, low % 2
    mid, top = rem(div(group + 1, 2), 2), div(group, 3)
    d = (mid * upper + top, mid * (1 - upper) + top, mid * (group - 1) + (1 - mid) * upper, core)
    return device_of(cube, tuple(m if isinstance(b, int) and b == 0 else rem(m + b, 2) for m, b in zip(member, d)))


def turn(x):
    quarter = jnp.floor(2.0 * x + 0.5)
    f = x - 0.5 * quarter
    f2 = f * f
    s = jnp.full_like(f, HALF_PI_TERMS_SIN[-1])
    for term in HALF_PI_TERMS_SIN[-2::-1]:
        s = s * f2 + np.float32(term)
    s = s * f
    c = jnp.full_like(f, HALF_PI_TERMS_COS[-1])
    for term in HALF_PI_TERMS_COS[-2::-1]:
        c = c * f2 + np.float32(term)
    half = jnp.floor(0.5 * quarter)
    odd = quarter - 2.0 * half
    sign = 1.0 - 2.0 * (half - 2.0 * jnp.floor(0.5 * half))
    is_odd = odd > 0.5
    return sign * jnp.where(is_odd, -s, c), sign * jnp.where(is_odd, c, s)


def times(a, b):
    return a[0] * b[0] - a[1] * b[1], a[0] * b[1] + a[1] * b[0]


def split(value):
    high = value.astype(BF16)
    return high, (value - high.astype(F32)).astype(BF16)


def fold(value):
    return jnp.sum(value, axis=0, keepdims=True)


def kernel(
    coef_a, coef_d, ids_a, ids_d, time_a, time_d, height, fill,
    out,
    turned, stage_a, stage_d, got_a, got_d, coefs,
    basis_a, basis_d, mine, theirs,
    weight_a, weight_d, err_a, err_d, y_a, y_d, vecs,
    part, ring_z, part_z, ring_xy, home_a, home_d,
    init_sem_a, init_sem_d, init_send, coef_sem, coef_send,
    swap_sem, swap_send, sum_sem, sum_send, home_sem, home_send,
):
    p, q = lax.axis_index("asc"), lax.axis_index("desc")
    cube, member = bits_of(p, q)
    me_class = 4 * cube[2] + 2 * cube[1] + cube[0]
    my_asc = asc_block(cube, member)
    my_h, my_q = desc_block(cube, member)
    my_i = me_class + 8 * my_h

    def at(cube_member):
        return device_of(*cube_member)

    barrier = pltpu.get_barrier_semaphore()

    def greet(device):
        pl.semaphore_signal(barrier, inc=1, device_id=device, device_id_type=MESH)

    for k in range(8):
        greet((my_asc, rem(q + k, 8)))
    for k in range(16):
        greet((rem(p + k, 16), my_q))
    for k in range(1, 16):
        greet(partner(cube, member, k // 4, k % 4))
    for k in range(1, 8):
        greet((p, rem(q + k, 8)))
    for k in range(1, 16):
        greet((rem(p + k, 16), q))
    greet(at(asc_home(q, p)))
    greet(at(desc_home(rem(p, 8), div(p, 8), q)))

    row = lax.broadcasted_iota(jnp.int32, (64, 128), 0)
    lane = lax.broadcasted_iota(jnp.int32, (64, 128), 1)
    fill_row = fill[...].astype(F32)
    fills = jnp.concatenate([fill_row, fill_row], axis=1)
    slot = (row + 64 * (lane // 64)).astype(F32)
    live = slot < fills
    sources = (
        (ids_a[...] % 32).astype(F32),
        time_a[...],
        height[...],
        (ids_d[...] % 32).astype(F32),
        time_d[...],
    )
    for k, source in enumerate(sources):
        both = jnp.concatenate([source, pltpu.roll(source, 64, 1)], axis=0)
        flat = both.T[0:64]
        turned[k] = jnp.where(live, flat, -1.0) if k in (0, 3) else flat
    for i in range(16):
        for k in range(3):
            stage_a[i, k] = turned[k, pl.ds(i, 4, stride=16), :]
        for k in range(2):
            stage_d[i, k] = turned[3 + k, pl.ds(i, 4, stride=16), :]

    sends = []
    for k in range(8):
        for kind, shift in ((0, q), (1, p)):
            j = rem(k + shift, 8)
            a_home = asc_home(j, p)
            for h in range(2):
                d_home = desc_home(j, h, q)
                r = slot_between(a_home[1], d_home[1])
                sends.append((kind, j + 8 * h, r, at(d_home) if kind else at(a_home)))
    home_of_a, home_of_d = at(asc_home(q, p)), at(desc_home(rem(p, 8), div(p, 8), q))

    pl.semaphore_wait(barrier, 8 + 16 + 15 + 7 + 15 + 2)

    def coef_copy(side, source, device):
        return pltpu.make_async_remote_copy(
            src_ref=source, dst_ref=coefs.at[side], send_sem=coef_send.at[side], recv_sem=coef_sem.at[side],
            device_id=device, device_id_type=MESH,
        )

    for kind, i, r, device in sends:
        stage, got, arrived = ((stage_a, got_a, init_sem_a), (stage_d, got_d, init_sem_d))[kind]
        pltpu.make_async_remote_copy(
            src_ref=stage.at[i], dst_ref=got.at[r], send_sem=init_send.at[kind], recv_sem=arrived.at[r],
            device_id=device, device_id_type=MESH,
        ).start()
    send_coef_a = coef_copy(0, coef_a, home_of_a)
    send_coef_d = coef_copy(1, coef_d, home_of_d)
    send_coef_a.start()
    send_coef_d.start()

    frequency = (lax.broadcasted_iota(jnp.int32, (8, 128), 0) + 1).astype(F32)
    arc = lax.broadcasted_iota(jnp.int32, (32, 128), 0).astype(F32)

    def make_basis(r, got, basis):
        for l in range(4):
            t = jnp.broadcast_to(got[r, 1, l : l + 1, :], (8, 128))
            first = turn(frequency * t)
            e8 = tuple(jnp.broadcast_to(v[7:8], (8, 128)) for v in first)
            e16 = times(e8, e8)
            e32 = times(e16, e16)
            blocks = [first, times(first, e8)]
            blocks += [times(b, e16) for b in blocks]
            blocks += [times(b, e32) for b in blocks]
            terms = jnp.concatenate([b[0] for b in blocks] + [b[1] for b in blocks], axis=0)
            high, low = split(terms)
            basis[r, 0:128, 128 * l : 128 * (l + 1)] = high
            basis[r, 128:256, 128 * l : 128 * (l + 1)] = low

    def left_of(vector):
        high, low = split(vector)
        return jnp.concatenate(
            [jnp.concatenate([high, high], axis=1), jnp.concatenate([low, low], axis=1)], axis=0
        )

    def apply(r, left, got, basis, kind, par, take_height):
        terms = jnp.dot(left, basis[r], preferred_element_type=F32)
        terms = terms[0:32] + terms[32:64]
        for l in range(4):
            ids = jnp.broadcast_to(got[r, 0, l : l + 1, :], (32, 128))
            line = fold(jnp.where(ids == arc, terms[:, 128 * l : 128 * (l + 1)], 0.0))
            if take_height:
                line = line - got[r, 2, l : l + 1, :]
            mine[par, r, kind, l : l + 1, :] = line

    def swap(par, high, low):
        device = partner(cube, member, high, low)
        r = 4 * high + low
        pltpu.make_async_remote_copy(
            src_ref=mine.at[par, r], dst_ref=theirs.at[par, r], send_sem=swap_send.at[par], recv_sem=swap_sem.at[par, r],
            device_id=device, device_id_type=MESH,
        ).start()

    def wait_swapped(par, r):
        pltpu.make_async_copy(theirs.at[par, r], theirs.at[par, r], swap_sem.at[par, r]).wait()

    def forward(par, vector, build=False, gathered=True):
        left_a, left_d = left_of(vector[0:32]), left_of(vector[32:64])

        def arrive(r):
            pltpu.make_async_copy(got_a.at[r], got_a.at[r], init_sem_a.at[r]).wait()
            pltpu.make_async_copy(got_d.at[r], got_d.at[r], init_sem_d.at[r]).wait()

        def four(high):
            for low in range(4 if build else 0):
                arrive(4 * high + low)
            for low in range(3, -1, -1):
                r = 4 * high + low
                if build:
                    make_basis(r, got_a, basis_a)
                    make_basis(r, got_d, basis_d)
                apply(r, left_a, got_a, basis_a, 0, par, build)
                apply(r, left_d, got_d, basis_d, 1, par, False)

        def step(k, carry):
            high = 3 - rem(2 * k, 3) if gathered else 3 - k
            four(high)
            for low in range(3, -1, -1):
                swap(par, high, low)
            return carry

        lax.fori_loop(0, 3, step, 0)
        four(0)
        for low in range(3, 0, -1):
            swap(par, 0, low)
        theirs[par, 0] = mine[par, 0]

    def collect(par, r, z, got):
        high = z.astype(BF16).astype(F32)
        low = z - high
        lines = []
        for l in range(4):
            hit = jnp.broadcast_to(got[r, 0, l : l + 1, :], (32, 128)) == arc
            both = [jnp.where(hit, jnp.broadcast_to(v[l : l + 1], (32, 128)), 0.0) for v in (high, low)]
            lines.append(jnp.concatenate(both, axis=0).astype(BF16))
        return jnp.concatenate(lines, axis=1)

    def contract(placed, basis):
        return lax.dot_general(placed, basis, (((1,), (1,)), ((), ())), preferred_element_type=F32)

    def unfold(total):
        return total[0:32, 0:128] + (total[0:32, 128:256] + total[32:64, 0:128]) + total[32:64, 128:256]

    def backward(par, react, arriving=True, between=None):
        def some(high, lows, carry):
            total_a, total_d = carry
            if arriving:
                for low in lows:
                    wait_swapped(par, 4 * high + low)
            for low in lows:
                r = 4 * high + low
                z_a, z_d = react(r)
                total_a += contract(collect(par, r, z_a, got_a), basis_a[r])
                total_d += contract(collect(par, r, z_d, got_d), basis_d[r])
            return total_a, total_d

        zero = jnp.zeros((64, 256), F32)
        z_a, z_d = react(0)
        carry = contract(collect(par, 0, z_a, got_a), basis_a[0]), contract(collect(par, 0, z_d, got_d), basis_d[0])
        carry = some(1, range(4), carry)
        if between:
            between()
        carry = some(0, range(1, 4), carry)
        for high in (2, 3):
            carry = some(high, range(4), carry)
        total_a, total_d = carry
        if arriving:
            wait_sent(par)
        return jnp.concatenate([unfold(total_a), unfold(total_d)], axis=0)

    def wait_sent(par):
        sent = mine.at[par, pl.ds(1, 15)]
        pltpu.make_async_copy(sent, sent, swap_send.at[par]).wait()

    def pairs(par, r):
        return mine[par, r, 0] - theirs[par, r, 1], theirs[par, r, 0] - mine[par, r, 1]

    def misfit(par, first):
        def react(r):
            if first:
                err_a[r], err_d[r] = pairs(par, r)
            zs = []
            for err, got, weight in ((err_a, got_a, weight_a), (err_d, got_d, weight_d)):
                lives = jnp.where(got[r, 0] >= 0.0, 1.0, 0.0)
                m = -lives * err[r]
                w = lives / (1.0 + m * m * INV_CAUCHY)
                weight[r] = w
                zs.append(w * m)
            return zs[0], -zs[1]

        return react

    def image(par, n):
        def react(r):
            a, d = pairs(par, r)
            y_a[n, r] = a
            y_d[n, r] = d
            return weight_a[r] * a, -(weight_d[r] * d)

        return react

    def take(par, n):
        lax.fori_loop(1, 16, lambda r, c: (wait_swapped(par, r), c)[1], 0)
        wait_sent(par)
        y_a[n] = mine[par, :, 0] - theirs[par, :, 1]
        y_d[n] = theirs[par, :, 0] - mine[par, :, 1]

    def sum_first(n, rows):
        rows = rows + [jnp.zeros((1, 128), F32)] * (8 - len(rows))
        sums = jnp.sum(jnp.concatenate(rows, axis=0), axis=1, keepdims=True)
        own = lax.broadcasted_iota(jnp.int32, (8, 128), 0) == lax.broadcasted_iota(jnp.int32, (8, 128), 1)
        line = fold(jnp.where(own, jnp.broadcast_to(sums, (8, 128)), 0.0))
        part[n] = line
        for k in (4, 3, 5, 2, 6, 1, 7):
            pltpu.make_async_remote_copy(
                src_ref=part.at[n], dst_ref=ring_z.at[n, q], send_sem=sum_send.at[n, 0], recv_sem=sum_sem.at[n, 0],
                device_id=(p, rem(q + k, 8)), device_id_type=MESH,
            ).start()
        ring_z[n, q] = line

    def added(ring, n, count):
        lines = [ring[n, k] for k in range(count)]
        while len(lines) > 1:
            lines = [a + b for a, b in zip(lines[0::2], lines[1::2])]
        return lines[0]

    def sum_second(n):
        whole = ring_z.at[n, pl.ds(0, 7)]
        pltpu.make_async_copy(whole, whole, sum_sem.at[n, 0]).wait()
        total = added(ring_z, n, 8)
        part_z[n] = total
        for k in (10, 6, 2, 14, 8, 9, 7, 5, 11, 3, 13, 1, 15, 4, 12):
            pltpu.make_async_remote_copy(
                src_ref=part_z.at[n], dst_ref=ring_xy.at[n, p], send_sem=sum_send.at[n, 1], recv_sem=sum_sem.at[n, 1],
                device_id=(rem(p + k, 16), q), device_id_type=MESH,
            ).start()
        ring_xy[n, p] = total

    def sum_last(n):
        whole = ring_xy.at[n, pl.ds(0, 15)]
        pltpu.make_async_copy(whole, whole, sum_sem.at[n, 1]).wait()
        total = added(ring_xy, n, 16)
        return [jnp.broadcast_to(total[:, k : k + 1], (1, 128)) for k in range(8)]

    def sum_sent(n):
        for stage, whole in ((0, ring_z.at[n, pl.ds(0, 7)]), (1, ring_xy.at[n, pl.ds(0, 15)])):
            pltpu.make_async_copy(whole, whole, sum_send.at[n, stage]).wait()

    def send_home(k):
        for side, buffer, device in ((0, home_a, (my_asc, me_class)), (1, home_d, (my_i, my_q))):
            pltpu.make_async_remote_copy(
                src_ref=vecs.at[k, pl.ds(32 * side, 32)], dst_ref=buffer.at[k],
                send_sem=home_send.at[side, k], recv_sem=home_sem.at[side, k],
                device_id=device, device_id_type=MESH,
            ).start()

    send_coef_a.wait_recv()
    send_coef_d.wait_recv()
    state = jnp.concatenate([coefs[0], coefs[1]], axis=0)
    par = 0
    forward(par, state, True)
    for step in range(2):
        last = step == 1
        vecs[0] = state
        if last:
            send_home(0)
        gradient = backward(par, misfit(par, not last), arriving=not last)
        if not last:
            par = 1 - par
        r0 = gradient - DAMPING * state
        vecs[1] = r0
        forward(par, r0)
        v1 = backward(par, image(par, 0)) + DAMPING * r0
        par = 1 - par
        vecs[2] = v1
        sum_first(2 * step, [fold(r0 * r0), fold(r0 * v1)])
        if last:
            send_home(1)
        forward(par, v1)
        v2 = backward(par, image(par, 1), between=functools.partial(sum_second, 2 * step)) + DAMPING * v1
        par = 1 - par
        vecs[3] = v2
        if last:
            send_home(2)
        forward(par, v2, gathered=False)
        rr0, mu0 = sum_last(2 * step)[0:2]
        a0 = rr0 / mu0
        r1 = r0 - a0 * v1
        u1 = v1 - a0 * v2
        lines = [fold(r1 * r1), fold(r1 * u1), fold(r1 * v1), fold(u1 * u1), fold(u1 * v1), fold(v1 * v1)]
        take(par, 2)
        par = 1 - par
        ju = y_a[1] - a0 * y_a[2]
        curve = jnp.sum(weight_a[...] * ju * ju, axis=0)
        sum_first(2 * step + 1, lines + [fold(curve)])
        if last:
            send_home(3)
        sum_second(2 * step + 1)
        rr1, ru, rv, uu, uv, vv, wuu = sum_last(2 * step + 1)[0:7]
        b1 = rr1 / rr0
        a1 = rr1 / (ru + 2.0 * b1 * rv + b1 * b1 * mu0)
        g1 = a1 * b1
        rr2 = rr1 + a1 * a1 * uu + g1 * g1 * vv - 2.0 * a1 * ru - 2.0 * g1 * rv + 2.0 * a1 * g1 * uv
        rr2 = jnp.maximum(rr2, 0.0)
        b2 = rr2 / rr1
        pr, pu, pv, p0 = 1.0 + b2, -a1, -g1, b2 * b1
        m_uu, m_uv, m_vv = wuu + 2.0 * uu, (uv - uu) / a0, (vv - uv) / a0
        curve2 = (
            pr * pr * ru + pu * pu * m_uu + pv * pv * m_vv + p0 * p0 * mu0
            + 2.0 * (pr * pu * uu + pr * pv * uv + pr * p0 * rv + pu * pv * m_uv + pu * p0 * uv + pv * p0 * vv)
        )
        a2 = rr2 / jnp.maximum(curve2, jnp.maximum(2.0 * rr2, 1e-30))
        c_r = a1 + a2 * pr
        c_u = a2 * pu
        k0 = a0 + g1 + a2 * p0 + c_r
        k1 = a2 * pv - a0 * c_r + c_u
        k2 = -a0 * c_u
        if not last:
            state = state + (k0 * r0 + k1 * v1 + k2 * v2)
            for err, y in ((err_a, y_a), (err_d, y_d)):
                err[...] = err[...] + (k0 * y[0] + k1 * y[1] + k2 * y[2])

    send_coef_a.wait_send()
    send_coef_d.wait_send()
    for n in range(4):
        sum_sent(n)
    pltpu.make_async_copy(stage_a, stage_a, init_send.at[0]).wait()
    pltpu.make_async_copy(stage_d, stage_d, init_send.at[1]).wait()
    for side, buffer in enumerate((home_a, home_d)):
        for k in range(4):
            pltpu.make_async_copy(buffer.at[k], buffer.at[k], home_sem.at[side, k]).wait()
            pltpu.make_async_copy(buffer.at[k], buffer.at[k], home_send.at[side, k]).wait()
        out[32 * side : 32 * side + 32] = buffer[0] + (k0 * buffer[1] + k1 * buffer[2] + k2 * buffer[3])


def body(coef_a, coef_d, cross_a, cross_d, time_a, time_d, height, fill):
    vmem = pl.BlockSpec(memory_space=pltpu.VMEM)
    values = pltpu.VMEM((SLOTS, 4, 128), F32)
    dma = pltpu.SemaphoreType.DMA
    out = pl.pallas_call(
        kernel,
        out_shape=jax.ShapeDtypeStruct((64, 128), F32),
        in_specs=[vmem] * 8,
        out_specs=vmem,
        scratch_shapes=[
            pltpu.VMEM((5, 64, 128), F32),
            pltpu.VMEM((16, 3, 4, 128), F32),
            pltpu.VMEM((16, 2, 4, 128), F32),
            pltpu.VMEM((SLOTS, 3, 4, 128), F32),
            pltpu.VMEM((SLOTS, 2, 4, 128), F32),
            pltpu.VMEM((2, 32, 128), F32),
            pltpu.VMEM((SLOTS, 256, 512), BF16),
            pltpu.VMEM((SLOTS, 256, 512), BF16),
            pltpu.VMEM((2, SLOTS, 2, 4, 128), F32),
            pltpu.VMEM((2, SLOTS, 2, 4, 128), F32),
            values,
            values,
            values,
            values,
            pltpu.VMEM((3, SLOTS, 4, 128), F32),
            pltpu.VMEM((3, SLOTS, 4, 128), F32),
            pltpu.VMEM((4, 64, 128), F32),
            pltpu.VMEM((4, 1, 128), F32),
            pltpu.VMEM((4, 8, 1, 128), F32),
            pltpu.VMEM((4, 1, 128), F32),
            pltpu.VMEM((4, 16, 1, 128), F32),
            pltpu.VMEM((4, 32, 128), F32),
            pltpu.VMEM((4, 32, 128), F32),
            dma((SLOTS,)),
            dma((SLOTS,)),
            dma((2,)),
            dma((2,)),
            dma((2,)),
            dma((2, SLOTS)),
            dma((2,)),
            dma((4, 2)),
            dma((4, 2)),
            dma((2, 4)),
            dma((2, 4)),
        ],
        compiler_params=pltpu.CompilerParams(collective_id=0, has_side_effects=True),
        name="adjust",
    )(coef_a, coef_d, cross_a, cross_d, time_a, time_d, height, fill.reshape(1, -1))
    return out[0:32], out[32:64]


def solution(mesh):
    rows = P(("asc", "desc"), None)
    return jax.shard_map(
        body,
        mesh=mesh,
        in_specs=(rows,) * 7 + (P(("asc", "desc")),),
        out_specs=(rows, rows),
        check_vma=False,
    )
```

```python
import functools

import jax
import jax.numpy as jnp
import numpy as np
from jax import lax
from jax.experimental import pallas as pl
from jax.experimental.pallas import tpu as pltpu
from jax.sharding import PartitionSpec as P

MESH = pl.DeviceIdType.MESH
F32 = jnp.float32
BF16 = jnp.bfloat16
DAMPING = 2.0
INV_CAUCHY = 1.0 / 2.25
SLOTS = 16
HALF_PI_TERMS_SIN = [np.pi**n * s / f for n, s, f in ((1, 1, 1), (3, -1, 6), (5, 1, 120), (7, -1, 5040), (9, 1, 362880), (11, -1, 39916800))]
HALF_PI_TERMS_COS = [np.pi**n * s / f for n, s, f in ((0, 1, 1), (2, -1, 2), (4, 1, 24), (6, -1, 720), (8, 1, 40320), (10, -1, 3628800))]


def div(a, n):
    return a // n if isinstance(a, int) else lax.div(a, jnp.int32(n))


def rem(a, n):
    return a % n if isinstance(a, int) else lax.rem(a, jnp.int32(n))


def bits_of(p, q):
    y, x, z, c = div(p, 4), rem(p, 4), div(q, 2), rem(q, 2)
    return (div(y, 2), div(x, 2), div(z, 2)), (rem(y, 2), rem(x, 2), rem(z, 2), c)


def cube_of(j):
    return (rem(j, 2), rem(div(j, 2), 2), div(j, 4))


def device_of(cube, member):
    return ((2 * cube[0] + member[0]) * 4 + 2 * cube[1] + member[1], (2 * cube[2] + member[2]) * 2 + member[3])


def asc_home(j, p):
    cube = cube_of(j)
    e = rem(div(p, 4) + 7 - 2 * cube[0], 4)
    f = rem(rem(p, 4) + 7 - 2 * cube[1], 4)
    return cube, (rem(e, 2), rem(f, 2), div(e, 2), div(f, 2))


def asc_block(cube, member):
    y = rem(2 * cube[0] + member[0] + 1 + 2 * member[2], 4)
    x = rem(2 * cube[1] + member[1] + 1 + 2 * member[3], 4)
    return y * 4 + x


def desc_home(j, h, q):
    cube = cube_of(j)
    e = rem(div(q, 2) + 7 - 2 * cube[2], 4)
    return cube, (rem(h + cube[0] + cube[2], 2), div(e, 2), rem(e, 2), rem(q, 2))


def desc_block(cube, member):
    z = rem(2 * cube[2] + member[2] + 1 + 2 * member[1], 4)
    h = rem(member[0] + cube[0] + cube[2], 2)
    return h, z * 2 + member[3]


def slot_between(first, second):
    dy, dx, dz, dc = [rem(a + b, 2) for a, b in zip(first, second)]
    mid = rem(dy + dx, 2)
    group = mid * (1 + dz) + (1 - mid) * 3 * dy
    return 4 * group + 2 * (mid * dy + (1 - mid) * dz) + dc


def partner(cube, member, group, low):
    upper, core = low // 2, low % 2
    mid, top = rem(div(group + 1, 2), 2), div(group, 3)
    d = (mid * upper + top, mid * (1 - upper) + top, mid * (group - 1) + (1 - mid) * upper, core)
    return device_of(cube, tuple(m if isinstance(b, int) and b == 0 else rem(m + b, 2) for m, b in zip(member, d)))


def turn(x):
    quarter = jnp.floor(2.0 * x + 0.5)
    f = x - 0.5 * quarter
    f2 = f * f
    s = jnp.full_like(f, HALF_PI_TERMS_SIN[-1])
    for term in HALF_PI_TERMS_SIN[-2::-1]:
        s = s * f2 + np.float32(term)
    s = s * f
    c = jnp.full_like(f, HALF_PI_TERMS_COS[-1])
    for term in HALF_PI_TERMS_COS[-2::-1]:
        c = c * f2 + np.float32(term)
    half = jnp.floor(0.5 * quarter)
    odd = quarter - 2.0 * half
    sign = 1.0 - 2.0 * (half - 2.0 * jnp.floor(0.5 * half))
    is_odd = odd > 0.5
    return sign * jnp.where(is_odd, -s, c), sign * jnp.where(is_odd, c, s)


def times(a, b):
    return a[0] * b[0] - a[1] * b[1], a[0] * b[1] + a[1] * b[0]


def split(value):
    high = value.astype(BF16)
    return high, (value - high.astype(F32)).astype(BF16)


def fold(value):
    return jnp.sum(value, axis=0, keepdims=True)


def kernel(
    coef_a, coef_d, ids_a, ids_d, time_a, time_d, height, fill,
    out,
    turned, stage_a, stage_d, got_a, got_d, coefs,
    basis_a, basis_d, mine, theirs,
    weight_a, weight_d, err_a, err_d, y_a, y_d, vecs,
    part, ring_z, part_z, ring_xy, home_a, home_d,
    init_sem_a, init_sem_d, init_send, coef_sem, coef_send,
    swap_sem, swap_send, sum_sem, sum_send, home_sem, home_send,
):
    p, q = lax.axis_index("asc"), lax.axis_index("desc")
    cube, member = bits_of(p, q)
    me_class = 4 * cube[2] + 2 * cube[1] + cube[0]
    my_asc = asc_block(cube, member)
    my_h, my_q = desc_block(cube, member)
    my_i = me_class + 8 * my_h

    def at(cube_member):
        return device_of(*cube_member)

    barrier = pltpu.get_barrier_semaphore()

    def greet(device):
        pl.semaphore_signal(barrier, inc=1, device_id=device, device_id_type=MESH)

    for k in range(8):
        greet((my_asc, rem(q + k, 8)))
    for k in range(16):
        greet((rem(p + k, 16), my_q))
    for k in range(1, 16):
        greet(partner(cube, member, k // 4, k % 4))
    for k in range(1, 8):
        greet((p, rem(q + k, 8)))
    for k in range(1, 16):
        greet((rem(p + k, 16), q))
    greet(at(asc_home(q, p)))
    greet(at(desc_home(rem(p, 8), div(p, 8), q)))

    row = lax.broadcasted_iota(jnp.int32, (64, 128), 0)
    lane = lax.broadcasted_iota(jnp.int32, (64, 128), 1)
    fill_row = fill[...].astype(F32)
    fills = jnp.concatenate([fill_row, fill_row], axis=1)
    slot = (row + 64 * (lane // 64)).astype(F32)
    live = slot < fills
    sources = (
        (ids_a[...] % 32).astype(F32),
        time_a[...],
        height[...],
        (ids_d[...] % 32).astype(F32),
        time_d[...],
    )
    for k, source in enumerate(sources):
        both = jnp.concatenate([source, pltpu.roll(source, 64, 1)], axis=0)
        flat = both.T[0:64]
        turned[k] = jnp.where(live, flat, -1.0) if k in (0, 3) else flat
    for i in range(16):
        for k in range(3):
            stage_a[i, k] = turned[k, pl.ds(i, 4, stride=16), :]
        for k in range(2):
            stage_d[i, k] = turned[3 + k, pl.ds(i, 4, stride=16), :]

    sends = []
    for k in range(8):
        for kind, shift in ((0, q), (1, p)):
            j = rem(k + shift, 8)
            a_home = asc_home(j, p)
            for h in range(2):
                d_home = desc_home(j, h, q)
                r = slot_between(a_home[1], d_home[1])
                sends.append((kind, j + 8 * h, r, at(d_home) if kind else at(a_home)))
    home_of_a, home_of_d = at(asc_home(q, p)), at(desc_home(rem(p, 8), div(p, 8), q))

    pl.semaphore_wait(barrier, 8 + 16 + 15 + 7 + 15 + 2)

    def coef_copy(side, source, device):
        return pltpu.make_async_remote_copy(
            src_ref=source, dst_ref=coefs.at[side], send_sem=coef_send.at[side], recv_sem=coef_sem.at[side],
            device_id=device, device_id_type=MESH,
        )

    for kind, i, r, device in sends:
        stage, got, arrived = ((stage_a, got_a, init_sem_a), (stage_d, got_d, init_sem_d))[kind]
        pltpu.make_async_remote_copy(
            src_ref=stage.at[i], dst_ref=got.at[r], send_sem=init_send.at[kind], recv_sem=arrived.at[r],
            device_id=device, device_id_type=MESH,
        ).start()
    send_coef_a = coef_copy(0, coef_a, home_of_a)
    send_coef_d = coef_copy(1, coef_d, home_of_d)
    send_coef_a.start()
    send_coef_d.start()

    frequency = (lax.broadcasted_iota(jnp.int32, (8, 128), 0) + 1).astype(F32)
    arc = lax.broadcasted_iota(jnp.int32, (32, 128), 0).astype(F32)

    def make_basis(r, got, basis):
        for l in range(4):
            t = jnp.broadcast_to(got[r, 1, l : l + 1, :], (8, 128))
            first = turn(frequency * t)
            e8 = tuple(jnp.broadcast_to(v[7:8], (8, 128)) for v in first)
            e16 = times(e8, e8)
            e32 = times(e16, e16)
            blocks = [first, times(first, e8)]
            blocks += [times(b, e16) for b in blocks]
            blocks += [times(b, e32) for b in blocks]
            terms = jnp.concatenate([b[0] for b in blocks] + [b[1] for b in blocks], axis=0)
            high, low = split(terms)
            basis[r, 0:128, 128 * l : 128 * (l + 1)] = high
            basis[r, 128:256, 128 * l : 128 * (l + 1)] = low

    def left_of(vector):
        high, low = split(vector)
        return jnp.concatenate(
            [jnp.concatenate([high, high], axis=1), jnp.concatenate([low, low], axis=1)], axis=0
        )

    def apply(r, left, got, basis, kind, par, take_height):
        terms = jnp.dot(left, basis[r], preferred_element_type=F32)
        terms = terms[0:32] + terms[32:64]
        for l in range(4):
            ids = jnp.broadcast_to(got[r, 0, l : l + 1, :], (32, 128))
            line = fold(jnp.where(ids == arc, terms[:, 128 * l : 128 * (l + 1)], 0.0))
            if take_height:
                line = line - got[r, 2, l : l + 1, :]
            mine[par, r, kind, l : l + 1, :] = line

    def swap(par, high, low):
        device = partner(cube, member, high, low)
        r = 4 * high + low
        pltpu.make_async_remote_copy(
            src_ref=mine.at[par, r], dst_ref=theirs.at[par, r], send_sem=swap_send.at[par], recv_sem=swap_sem.at[par, r],
            device_id=device, device_id_type=MESH,
        ).start()

    def wait_swapped(par, r):
        pltpu.make_async_copy(theirs.at[par, r], theirs.at[par, r], swap_sem.at[par, r]).wait()

    def forward(par, vector, build=False, gathered=True):
        left_a, left_d = left_of(vector[0:32]), left_of(vector[32:64])

        def arrive(r):
            pltpu.make_async_copy(got_a.at[r], got_a.at[r], init_sem_a.at[r]).wait()
            pltpu.make_async_copy(got_d.at[r], got_d.at[r], init_sem_d.at[r]).wait()

        def four(high):
            for low in range(4 if build else 0):
                arrive(4 * high + low)
            for low in range(3, -1, -1):
                r = 4 * high + low
                if build:
                    make_basis(r, got_a, basis_a)
                    make_basis(r, got_d, basis_d)
                apply(r, left_a, got_a, basis_a, 0, par, build)
                apply(r, left_d, got_d, basis_d, 1, par, False)

        for high in (3, 1, 0, 2):
            four(high)
            for low in range(3, -1 if high else 0, -1):
                swap(par, high, low)
        theirs[par, 0] = mine[par, 0]

    def collect(par, r, z, got):
        high = z.astype(BF16).astype(F32)
        low = z - high
        lines = []
        for l in range(4):
            hit = jnp.broadcast_to(got[r, 0, l : l + 1, :], (32, 128)) == arc
            both = [jnp.where(hit, jnp.broadcast_to(v[l : l + 1], (32, 128)), 0.0) for v in (high, low)]
            lines.append(jnp.concatenate(both, axis=0).astype(BF16))
        return jnp.concatenate(lines, axis=1)

    def contract(placed, basis):
        return lax.dot_general(placed, basis, (((1,), (1,)), ((), ())), preferred_element_type=F32)

    def unfold(total):
        return total[0:32, 0:128] + (total[0:32, 128:256] + total[32:64, 0:128]) + total[32:64, 128:256]

    def backward(par, react, arriving=True, between=None):
        def some(high, lows, carry):
            total_a, total_d = carry
            if arriving:
                for low in lows:
                    wait_swapped(par, 4 * high + low)
            for low in lows:
                r = 4 * high + low
                z_a, z_d = react(r)
                total_a += contract(collect(par, r, z_a, got_a), basis_a[r])
                total_d += contract(collect(par, r, z_d, got_d), basis_d[r])
            return total_a, total_d

        zero = jnp.zeros((64, 256), F32)
        z_a, z_d = react(0)
        carry = contract(collect(par, 0, z_a, got_a), basis_a[0]), contract(collect(par, 0, z_d, got_d), basis_d[0])
        carry = some(1, range(4), carry)
        if between:
            between()
        carry = some(0, range(1, 4), carry)
        for high in (3, 2):
            carry = some(high, range(4), carry)
        total_a, total_d = carry
        if arriving:
            wait_sent(par)
        return jnp.concatenate([unfold(total_a), unfold(total_d)], axis=0)

    def wait_sent(par):
        sent = mine.at[par, pl.ds(1, 15)]
        pltpu.make_async_copy(sent, sent, swap_send.at[par]).wait()

    def pairs(par, r):
        return mine[par, r, 0] - theirs[par, r, 1], theirs[par, r, 0] - mine[par, r, 1]

    def misfit(par, first):
        def react(r):
            if first:
                err_a[r], err_d[r] = pairs(par, r)
            zs = []
            for err, got, weight in ((err_a, got_a, weight_a), (err_d, got_d, weight_d)):
                lives = jnp.where(got[r, 0] >= 0.0, 1.0, 0.0)
                m = -lives * err[r]
                w = lives / (1.0 + m * m * INV_CAUCHY)
                weight[r] = w
                zs.append(w * m)
            return zs[0], -zs[1]

        return react

    def image(par, n):
        def react(r):
            a, d = pairs(par, r)
            y_a[n, r] = a
            y_d[n, r] = d
            return weight_a[r] * a, -(weight_d[r] * d)

        return react

    def take(par, n):
        lax.fori_loop(1, 16, lambda r, c: (wait_swapped(par, r), c)[1], 0)
        wait_sent(par)
        y_a[n] = mine[par, :, 0] - theirs[par, :, 1]
        y_d[n] = theirs[par, :, 0] - mine[par, :, 1]

    def sum_first(n, rows):
        rows = rows + [jnp.zeros((1, 128), F32)] * (8 - len(rows))
        sums = jnp.sum(jnp.concatenate(rows, axis=0), axis=1, keepdims=True)
        own = lax.broadcasted_iota(jnp.int32, (8, 128), 0) == lax.broadcasted_iota(jnp.int32, (8, 128), 1)
        line = fold(jnp.where(own, jnp.broadcast_to(sums, (8, 128)), 0.0))
        part[n] = line
        for k in (4, 3, 5, 2, 6, 1, 7):
            pltpu.make_async_remote_copy(
                src_ref=part.at[n], dst_ref=ring_z.at[n, q], send_sem=sum_send.at[n, 0], recv_sem=sum_sem.at[n, 0],
                device_id=(p, rem(q + k, 8)), device_id_type=MESH,
            ).start()
        ring_z[n, q] = line

    def added(ring, n, count):
        lines = [ring[n, k] for k in range(count)]
        while len(lines) > 1:
            lines = [a + b for a, b in zip(lines[0::2], lines[1::2])]
        return lines[0]

    def sum_second(n):
        whole = ring_z.at[n, pl.ds(0, 7)]
        pltpu.make_async_copy(whole, whole, sum_sem.at[n, 0]).wait()
        total = added(ring_z, n, 8)
        part_z[n] = total
        for k in (10, 6, 2, 14, 8, 9, 7, 5, 11, 3, 13, 1, 15, 4, 12):
            pltpu.make_async_remote_copy(
                src_ref=part_z.at[n], dst_ref=ring_xy.at[n, p], send_sem=sum_send.at[n, 1], recv_sem=sum_sem.at[n, 1],
                device_id=(rem(p + k, 16), q), device_id_type=MESH,
            ).start()
        ring_xy[n, p] = total

    def sum_last(n):
        whole = ring_xy.at[n, pl.ds(0, 15)]
        pltpu.make_async_copy(whole, whole, sum_sem.at[n, 1]).wait()
        total = added(ring_xy, n, 16)
        return [jnp.broadcast_to(total[:, k : k + 1], (1, 128)) for k in range(8)]

    def sum_sent(n):
        for stage, whole in ((0, ring_z.at[n, pl.ds(0, 7)]), (1, ring_xy.at[n, pl.ds(0, 15)])):
            pltpu.make_async_copy(whole, whole, sum_send.at[n, stage]).wait()

    def send_home(k):
        for side, buffer, device in ((0, home_a, (my_asc, me_class)), (1, home_d, (my_i, my_q))):
            pltpu.make_async_remote_copy(
                src_ref=vecs.at[k, pl.ds(32 * side, 32)], dst_ref=buffer.at[k],
                send_sem=home_send.at[side, k], recv_sem=home_sem.at[side, k],
                device_id=device, device_id_type=MESH,
            ).start()

    send_coef_a.wait_recv()
    send_coef_d.wait_recv()
    state = jnp.concatenate([coefs[0], coefs[1]], axis=0)
    par = 0
    forward(par, state, True)
    for step in range(2):
        last = step == 1
        vecs[0] = state
        if last:
            send_home(0)
        gradient = backward(par, misfit(par, not last), arriving=not last)
        if not last:
            par = 1 - par
        r0 = gradient - DAMPING * state
        vecs[1] = r0
        forward(par, r0)
        v1 = backward(par, image(par, 0)) + DAMPING * r0
        par = 1 - par
        vecs[2] = v1
        sum_first(2 * step, [fold(r0 * r0), fold(r0 * v1)])
        if last:
            send_home(1)
        forward(par, v1)
        v2 = backward(par, image(par, 1), between=functools.partial(sum_second, 2 * step)) + DAMPING * v1
        par = 1 - par
        vecs[3] = v2
        if last:
            send_home(2)
        forward(par, v2, gathered=False)
        rr0, mu0 = sum_last(2 * step)[0:2]
        a0 = rr0 / mu0
        r1 = r0 - a0 * v1
        u1 = v1 - a0 * v2
        lines = [fold(r1 * r1), fold(r1 * u1), fold(r1 * v1), fold(u1 * u1), fold(u1 * v1), fold(v1 * v1)]
        take(par, 2)
        par = 1 - par
        ju = y_a[1] - a0 * y_a[2]
        curve = jnp.sum(weight_a[...] * ju * ju, axis=0)
        sum_first(2 * step + 1, lines + [fold(curve)])
        if last:
            send_home(3)
        sum_second(2 * step + 1)
        rr1, ru, rv, uu, uv, vv, wuu = sum_last(2 * step + 1)[0:7]
        b1 = rr1 / rr0
        a1 = rr1 / (ru + 2.0 * b1 * rv + b1 * b1 * mu0)
        g1 = a1 * b1
        rr2 = rr1 + a1 * a1 * uu + g1 * g1 * vv - 2.0 * a1 * ru - 2.0 * g1 * rv + 2.0 * a1 * g1 * uv
        rr2 = jnp.maximum(rr2, 0.0)
        b2 = rr2 / rr1
        pr, pu, pv, p0 = 1.0 + b2, -a1, -g1, b2 * b1
        m_uu, m_uv, m_vv = wuu + 2.0 * uu, (uv - uu) / a0, (vv - uv) / a0
        curve2 = (
            pr * pr * ru + pu * pu * m_uu + pv * pv * m_vv + p0 * p0 * mu0
            + 2.0 * (pr * pu * uu + pr * pv * uv + pr * p0 * rv + pu * pv * m_uv + pu * p0 * uv + pv * p0 * vv)
        )
        a2 = rr2 / jnp.maximum(curve2, jnp.maximum(2.0 * rr2, 1e-30))
        c_r = a1 + a2 * pr
        c_u = a2 * pu
        k0 = a0 + g1 + a2 * p0 + c_r
        k1 = a2 * pv - a0 * c_r + c_u
        k2 = -a0 * c_u
        if not last:
            state = state + (k0 * r0 + k1 * v1 + k2 * v2)
            for err, y in ((err_a, y_a), (err_d, y_d)):
                err[...] = err[...] + (k0 * y[0] + k1 * y[1] + k2 * y[2])

    send_coef_a.wait_send()
    send_coef_d.wait_send()
    for n in range(4):
        sum_sent(n)
    pltpu.make_async_copy(stage_a, stage_a, init_send.at[0]).wait()
    pltpu.make_async_copy(stage_d, stage_d, init_send.at[1]).wait()
    for side, buffer in enumerate((home_a, home_d)):
        for k in range(4):
            pltpu.make_async_copy(buffer.at[k], buffer.at[k], home_sem.at[side, k]).wait()
            pltpu.make_async_copy(buffer.at[k], buffer.at[k], home_send.at[side, k]).wait()
        out[32 * side : 32 * side + 32] = buffer[0] + (k0 * buffer[1] + k1 * buffer[2] + k2 * buffer[3])


def body(coef_a, coef_d, cross_a, cross_d, time_a, time_d, height, fill):
    vmem = pl.BlockSpec(memory_space=pltpu.VMEM)
    values = pltpu.VMEM((SLOTS, 4, 128), F32)
    dma = pltpu.SemaphoreType.DMA
    out = pl.pallas_call(
        kernel,
        out_shape=jax.ShapeDtypeStruct((64, 128), F32),
        in_specs=[vmem] * 8,
        out_specs=vmem,
        scratch_shapes=[
            pltpu.VMEM((5, 64, 128), F32),
            pltpu.VMEM((16, 3, 4, 128), F32),
            pltpu.VMEM((16, 2, 4, 128), F32),
            pltpu.VMEM((SLOTS, 3, 4, 128), F32),
            pltpu.VMEM((SLOTS, 2, 4, 128), F32),
            pltpu.VMEM((2, 32, 128), F32),
            pltpu.VMEM((SLOTS, 256, 512), BF16),
            pltpu.VMEM((SLOTS, 256, 512), BF16),
            pltpu.VMEM((2, SLOTS, 2, 4, 128), F32),
            pltpu.VMEM((2, SLOTS, 2, 4, 128), F32),
            values,
            values,
            values,
            values,
            pltpu.VMEM((3, SLOTS, 4, 128), F32),
            pltpu.VMEM((3, SLOTS, 4, 128), F32),
            pltpu.VMEM((4, 64, 128), F32),
            pltpu.VMEM((4, 1, 128), F32),
            pltpu.VMEM((4, 8, 1, 128), F32),
            pltpu.VMEM((4, 1, 128), F32),
            pltpu.VMEM((4, 16, 1, 128), F32),
            pltpu.VMEM((4, 32, 128), F32),
            pltpu.VMEM((4, 32, 128), F32),
            dma((SLOTS,)),
            dma((SLOTS,)),
            dma((2,)),
            dma((2,)),
            dma((2,)),
            dma((2, SLOTS)),
            dma((2,)),
            dma((4, 2)),
            dma((4, 2)),
            dma((2, 4)),
            dma((2, 4)),
        ],
        compiler_params=pltpu.CompilerParams(collective_id=0, has_side_effects=True),
        name="adjust",
    )(coef_a, coef_d, cross_a, cross_d, time_a, time_d, height, fill.reshape(1, -1))
    return out[0:32], out[32:64]


def solution(mesh):
    rows = P(("asc", "desc"), None)
    return jax.shard_map(
        body,
        mesh=mesh,
        in_specs=(rows,) * 7 + (P(("asc", "desc")),),
        out_specs=(rows, rows),
        check_vma=False,
    )
```

```python
import functools

import jax
import jax.numpy as jnp
import numpy as np
from jax import lax
from jax.experimental import pallas as pl
from jax.experimental.pallas import tpu as pltpu
from jax.sharding import PartitionSpec as P

MESH = pl.DeviceIdType.MESH
F32 = jnp.float32
BF16 = jnp.bfloat16
DAMPING = 2.0
INV_CAUCHY = 1.0 / 2.25
SLOTS = 16
HALF_PI_TERMS_SIN = [np.pi**n * s / f for n, s, f in ((1, 1, 1), (3, -1, 6), (5, 1, 120), (7, -1, 5040), (9, 1, 362880), (11, -1, 39916800))]
HALF_PI_TERMS_COS = [np.pi**n * s / f for n, s, f in ((0, 1, 1), (2, -1, 2), (4, 1, 24), (6, -1, 720), (8, 1, 40320), (10, -1, 3628800))]


def div(a, n):
    return a // n if isinstance(a, int) else lax.div(a, jnp.int32(n))


def rem(a, n):
    return a % n if isinstance(a, int) else lax.rem(a, jnp.int32(n))


def bits_of(p, q):
    y, x, z, c = div(p, 4), rem(p, 4), div(q, 2), rem(q, 2)
    return (div(y, 2), div(x, 2), div(z, 2)), (rem(y, 2), rem(x, 2), rem(z, 2), c)


def cube_of(j):
    return (rem(j, 2), rem(div(j, 2), 2), div(j, 4))


def device_of(cube, member):
    return ((2 * cube[0] + member[0]) * 4 + 2 * cube[1] + member[1], (2 * cube[2] + member[2]) * 2 + member[3])


def asc_home(j, p):
    cube = cube_of(j)
    e = rem(div(p, 4) + 7 - 2 * cube[0], 4)
    f = rem(rem(p, 4) + 7 - 2 * cube[1], 4)
    return cube, (rem(e, 2), rem(f, 2), div(e, 2), div(f, 2))


def asc_block(cube, member):
    y = rem(2 * cube[0] + member[0] + 1 + 2 * member[2], 4)
    x = rem(2 * cube[1] + member[1] + 1 + 2 * member[3], 4)
    return y * 4 + x


def desc_home(j, h, q):
    cube = cube_of(j)
    e = rem(div(q, 2) + 7 - 2 * cube[2], 4)
    return cube, (rem(h + cube[0] + cube[2], 2), div(e, 2), rem(e, 2), rem(q, 2))


def desc_block(cube, member):
    z = rem(2 * cube[2] + member[2] + 1 + 2 * member[1], 4)
    h = rem(member[0] + cube[0] + cube[2], 2)
    return h, z * 2 + member[3]


def slot_between(first, second):
    dy, dx, dz, dc = [rem(a + b, 2) for a, b in zip(first, second)]
    mid = rem(dy + dx, 2)
    group = mid * (1 + dz) + (1 - mid) * 3 * dy
    return 4 * group + 2 * (mid * dy + (1 - mid) * dz) + dc


def partner(cube, member, group, low):
    upper, core = low // 2, low % 2
    mid, top = rem(div(group + 1, 2), 2), div(group, 3)
    d = (mid * upper + top, mid * (1 - upper) + top, mid * (group - 1) + (1 - mid) * upper, core)
    return device_of(cube, tuple(m if isinstance(b, int) and b == 0 else rem(m + b, 2) for m, b in zip(member, d)))


def turn(x):
    quarter = jnp.floor(2.0 * x + 0.5)
    f = x - 0.5 * quarter
    f2 = f * f
    s = jnp.full_like(f, HALF_PI_TERMS_SIN[-1])
    for term in HALF_PI_TERMS_SIN[-2::-1]:
        s = s * f2 + np.float32(term)
    s = s * f
    c = jnp.full_like(f, HALF_PI_TERMS_COS[-1])
    for term in HALF_PI_TERMS_COS[-2::-1]:
        c = c * f2 + np.float32(term)
    half = jnp.floor(0.5 * quarter)
    odd = quarter - 2.0 * half
    sign = 1.0 - 2.0 * (half - 2.0 * jnp.floor(0.5 * half))
    is_odd = odd > 0.5
    return sign * jnp.where(is_odd, -s, c), sign * jnp.where(is_odd, c, s)


def times(a, b):
    return a[0] * b[0] - a[1] * b[1], a[0] * b[1] + a[1] * b[0]


def split(value):
    high = value.astype(BF16)
    return high, (value - high.astype(F32)).astype(BF16)


def fold(value):
    return jnp.sum(value, axis=0, keepdims=True)


def kernel(
    coef_a, coef_d, ids_a, ids_d, time_a, time_d, height, fill,
    out,
    turned, stage_a, stage_d, got_a, got_d, coefs,
    basis_a, basis_d, mine, theirs,
    weight_a, weight_d, err_a, err_d, y_a, y_d, vecs,
    part, ring_z, part_z, ring_xy, home_a, home_d,
    init_sem_a, init_sem_d, init_send, coef_sem, coef_send,
    swap_sem, swap_send, sum_sem, sum_send, home_sem, home_send,
):
    p, q = lax.axis_index("asc"), lax.axis_index("desc")
    cube, member = bits_of(p, q)
    me_class = 4 * cube[2] + 2 * cube[1] + cube[0]
    my_asc = asc_block(cube, member)
    my_h, my_q = desc_block(cube, member)
    my_i = me_class + 8 * my_h

    def at(cube_member):
        return device_of(*cube_member)

    barrier = pltpu.get_barrier_semaphore()

    def greet(device):
        pl.semaphore_signal(barrier, inc=1, device_id=device, device_id_type=MESH)

    for k in range(8):
        greet((my_asc, rem(q + k, 8)))
    for k in range(16):
        greet((rem(p + k, 16), my_q))
    for k in range(1, 16):
        greet(partner(cube, member, k // 4, k % 4))
    for k in range(1, 8):
        greet((p, rem(q + k, 8)))
    for k in range(1, 16):
        greet((rem(p + k, 16), q))
    greet(at(asc_home(q, p)))
    greet(at(desc_home(rem(p, 8), div(p, 8), q)))

    row = lax.broadcasted_iota(jnp.int32, (64, 128), 0)
    lane = lax.broadcasted_iota(jnp.int32, (64, 128), 1)
    fill_row = fill[...].astype(F32)
    fills = jnp.concatenate([fill_row, fill_row], axis=1)
    slot = (row + 64 * (lane // 64)).astype(F32)
    live = slot < fills
    sources = (
        (ids_a[...] % 32).astype(F32),
        time_a[...],
        height[...],
        (ids_d[...] % 32).astype(F32),
        time_d[...],
    )
    for k, source in enumerate(sources):
        both = jnp.concatenate([source, pltpu.roll(source, 64, 1)], axis=0)
        flat = both.T[0:64]
        turned[k] = jnp.where(live, flat, -1.0) if k in (0, 3) else flat
    for i in range(16):
        for k in range(3):
            stage_a[i, k] = turned[k, pl.ds(i, 4, stride=16), :]
        for k in range(2):
            stage_d[i, k] = turned[3 + k, pl.ds(i, 4, stride=16), :]

    sends = []
    for k in range(8):
        for kind, shift in ((0, q), (1, p)):
            j = rem(k + shift, 8)
            a_home = asc_home(j, p)
            for h in range(2):
                d_home = desc_home(j, h, q)
                r = slot_between(a_home[1], d_home[1])
                sends.append((kind, j + 8 * h, r, at(d_home) if kind else at(a_home)))
    home_of_a, home_of_d = at(asc_home(q, p)), at(desc_home(rem(p, 8), div(p, 8), q))

    pl.semaphore_wait(barrier, 8 + 16 + 15 + 7 + 15 + 2)

    def coef_copy(side, source, device):
        return pltpu.make_async_remote_copy(
            src_ref=source, dst_ref=coefs.at[side], send_sem=coef_send.at[side], recv_sem=coef_sem.at[side],
            device_id=device, device_id_type=MESH,
        )

    for kind, i, r, device in sends:
        stage, got, arrived = ((stage_a, got_a, init_sem_a), (stage_d, got_d, init_sem_d))[kind]
        pltpu.make_async_remote_copy(
            src_ref=stage.at[i], dst_ref=got.at[r], send_sem=init_send.at[kind], recv_sem=arrived.at[r],
            device_id=device, device_id_type=MESH,
        ).start()
    send_coef_a = coef_copy(0, coef_a, home_of_a)
    send_coef_d = coef_copy(1, coef_d, home_of_d)
    send_coef_a.start()
    send_coef_d.start()

    frequency = (lax.broadcasted_iota(jnp.int32, (8, 128), 0) + 1).astype(F32)
    arc = lax.broadcasted_iota(jnp.int32, (32, 128), 0).astype(F32)

    def make_basis(r, got, basis):
        for l in range(4):
            t = jnp.broadcast_to(got[r, 1, l : l + 1, :], (8, 128))
            first = turn(frequency * t)
            e8 = tuple(jnp.broadcast_to(v[7:8], (8, 128)) for v in first)
            e16 = times(e8, e8)
            e32 = times(e16, e16)
            blocks = [first, times(first, e8)]
            blocks += [times(b, e16) for b in blocks]
            blocks += [times(b, e32) for b in blocks]
            terms = jnp.concatenate([b[0] for b in blocks] + [b[1] for b in blocks], axis=0)
            high, low = split(terms)
            basis[r, 0:128, 128 * l : 128 * (l + 1)] = high
            basis[r, 128:256, 128 * l : 128 * (l + 1)] = low

    def left_of(vector):
        high, low = split(vector)
        return jnp.concatenate(
            [jnp.concatenate([high, high], axis=1), jnp.concatenate([low, low], axis=1)], axis=0
        )

    def apply(r, left, got, basis, kind, par, take_height):
        terms = jnp.dot(left, basis[r], preferred_element_type=F32)
        terms = terms[0:32] + terms[32:64]
        for l in range(4):
            ids = jnp.broadcast_to(got[r, 0, l : l + 1, :], (32, 128))
            line = fold(jnp.where(ids == arc, terms[:, 128 * l : 128 * (l + 1)], 0.0))
            if take_height:
                line = line - got[r, 2, l : l + 1, :]
            mine[par, r, kind, l : l + 1, :] = line

    def swap(par, high, low):
        device = partner(cube, member, high, low)
        r = 4 * high + low
        pltpu.make_async_remote_copy(
            src_ref=mine.at[par, r], dst_ref=theirs.at[par, r], send_sem=swap_send.at[par], recv_sem=swap_sem.at[par, r],
            device_id=device, device_id_type=MESH,
        ).start()

    def wait_swapped(par, r):
        pltpu.make_async_copy(theirs.at[par, r], theirs.at[par, r], swap_sem.at[par, r]).wait()

    def forward(par, vector, build=False, gathered=True):
        left_a, left_d = left_of(vector[0:32]), left_of(vector[32:64])

        def arrive(r):
            pltpu.make_async_copy(got_a.at[r], got_a.at[r], init_sem_a.at[r]).wait()
            pltpu.make_async_copy(got_d.at[r], got_d.at[r], init_sem_d.at[r]).wait()

        def four(high):
            for low in range(4 if build else 0):
                arrive(4 * high + low)
            for low in range(3, -1, -1):
                r = 4 * high + low
                if build:
                    make_basis(r, got_a, basis_a)
                    make_basis(r, got_d, basis_d)
                apply(r, left_a, got_a, basis_a, 0, par, build)
                apply(r, left_d, got_d, basis_d, 1, par, False)

        for high in (3, 1, 0, 2) if gathered else (3, 2, 1, 0):
            four(high)
            for low in range(3, -1 if high else 0, -1):
                swap(par, high, low)
        theirs[par, 0] = mine[par, 0]

    def collect(par, r, z, got):
        high = z.astype(BF16).astype(F32)
        low = z - high
        lines = []
        for l in range(4):
            hit = jnp.broadcast_to(got[r, 0, l : l + 1, :], (32, 128)) == arc
            both = [jnp.where(hit, jnp.broadcast_to(v[l : l + 1], (32, 128)), 0.0) for v in (high, low)]
            lines.append(jnp.concatenate(both, axis=0).astype(BF16))
        return jnp.concatenate(lines, axis=1)

    def contract(placed, basis):
        return lax.dot_general(placed, basis, (((1,), (1,)), ((), ())), preferred_element_type=F32)

    def unfold(total):
        return total[0:32, 0:128] + (total[0:32, 128:256] + total[32:64, 0:128]) + total[32:64, 128:256]

    def backward(par, react, arriving=True, between=None):
        def some(high, lows, carry):
            total_a, total_d = carry
            if arriving:
                for low in lows:
                    wait_swapped(par, 4 * high + low)
            for low in lows:
                r = 4 * high + low
                z_a, z_d = react(r)
                total_a += contract(collect(par, r, z_a, got_a), basis_a[r])
                total_d += contract(collect(par, r, z_d, got_d), basis_d[r])
            return total_a, total_d

        zero = jnp.zeros((64, 256), F32)
        z_a, z_d = react(0)
        carry = contract(collect(par, 0, z_a, got_a), basis_a[0]), contract(collect(par, 0, z_d, got_d), basis_d[0])
        carry = some(1, range(4), carry)
        if between:
            between()
        carry = some(0, range(1, 4), carry)
        for high in (3, 2):
            carry = some(high, range(4), carry)
        total_a, total_d = carry
        if arriving:
            wait_sent(par)
        return jnp.concatenate([unfold(total_a), unfold(total_d)], axis=0)

    def wait_sent(par):
        sent = mine.at[par, pl.ds(1, 15)]
        pltpu.make_async_copy(sent, sent, swap_send.at[par]).wait()

    def pairs(par, r):
        return mine[par, r, 0] - theirs[par, r, 1], theirs[par, r, 0] - mine[par, r, 1]

    def misfit(par, first):
        def react(r):
            if first:
                err_a[r], err_d[r] = pairs(par, r)
            zs = []
            for err, got, weight in ((err_a, got_a, weight_a), (err_d, got_d, weight_d)):
                lives = jnp.where(got[r, 0] >= 0.0, 1.0, 0.0)
                m = -lives * err[r]
                w = lives / (1.0 + m * m * INV_CAUCHY)
                weight[r] = w
                zs.append(w * m)
            return zs[0], -zs[1]

        return react

    def image(par, n):
        def react(r):
            a, d = pairs(par, r)
            y_a[n, r] = a
            y_d[n, r] = d
            return weight_a[r] * a, -(weight_d[r] * d)

        return react

    def take(par, n):
        lax.fori_loop(1, 16, lambda r, c: (wait_swapped(par, r), c)[1], 0)
        wait_sent(par)
        y_a[n] = mine[par, :, 0] - theirs[par, :, 1]
        y_d[n] = theirs[par, :, 0] - mine[par, :, 1]

    def sum_first(n, rows):
        rows = rows + [jnp.zeros((1, 128), F32)] * (8 - len(rows))
        sums = jnp.sum(jnp.concatenate(rows, axis=0), axis=1, keepdims=True)
        own = lax.broadcasted_iota(jnp.int32, (8, 128), 0) == lax.broadcasted_iota(jnp.int32, (8, 128), 1)
        line = fold(jnp.where(own, jnp.broadcast_to(sums, (8, 128)), 0.0))
        part[n] = line
        for k in (4, 3, 5, 2, 6, 1, 7):
            pltpu.make_async_remote_copy(
                src_ref=part.at[n], dst_ref=ring_z.at[n, q], send_sem=sum_send.at[n, 0], recv_sem=sum_sem.at[n, 0],
                device_id=(p, rem(q + k, 8)), device_id_type=MESH,
            ).start()
        ring_z[n, q] = line

    def added(ring, n, count):
        lines = [ring[n, k] for k in range(count)]
        while len(lines) > 1:
            lines = [a + b for a, b in zip(lines[0::2], lines[1::2])]
        return lines[0]

    def sum_second(n):
        whole = ring_z.at[n, pl.ds(0, 7)]
        pltpu.make_async_copy(whole, whole, sum_sem.at[n, 0]).wait()
        total = added(ring_z, n, 8)
        part_z[n] = total
        for k in (10, 6, 2, 14, 8, 9, 7, 5, 11, 3, 13, 1, 15, 4, 12):
            pltpu.make_async_remote_copy(
                src_ref=part_z.at[n], dst_ref=ring_xy.at[n, p], send_sem=sum_send.at[n, 1], recv_sem=sum_sem.at[n, 1],
                device_id=(rem(p + k, 16), q), device_id_type=MESH,
            ).start()
        ring_xy[n, p] = total

    def sum_last(n):
        whole = ring_xy.at[n, pl.ds(0, 15)]
        pltpu.make_async_copy(whole, whole, sum_sem.at[n, 1]).wait()
        total = added(ring_xy, n, 16)
        return [jnp.broadcast_to(total[:, k : k + 1], (1, 128)) for k in range(8)]

    def sum_sent(n):
        for stage, whole in ((0, ring_z.at[n, pl.ds(0, 7)]), (1, ring_xy.at[n, pl.ds(0, 15)])):
            pltpu.make_async_copy(whole, whole, sum_send.at[n, stage]).wait()

    def send_home(k):
        for side, buffer, device in ((0, home_a, (my_asc, me_class)), (1, home_d, (my_i, my_q))):
            pltpu.make_async_remote_copy(
                src_ref=vecs.at[k, pl.ds(32 * side, 32)], dst_ref=buffer.at[k],
                send_sem=home_send.at[side, k], recv_sem=home_sem.at[side, k],
                device_id=device, device_id_type=MESH,
            ).start()

    send_coef_a.wait_recv()
    send_coef_d.wait_recv()
    state = jnp.concatenate([coefs[0], coefs[1]], axis=0)
    par = 0
    forward(par, state, True)
    for step in range(2):
        last = step == 1
        vecs[0] = state
        if last:
            send_home(0)
        gradient = backward(par, misfit(par, not last), arriving=not last)
        if not last:
            par = 1 - par
        r0 = gradient - DAMPING * state
        vecs[1] = r0
        forward(par, r0)
        v1 = backward(par, image(par, 0)) + DAMPING * r0
        par = 1 - par
        vecs[2] = v1
        sum_first(2 * step, [fold(r0 * r0), fold(r0 * v1)])
        if last:
            send_home(1)
        forward(par, v1)
        v2 = backward(par, image(par, 1), between=functools.partial(sum_second, 2 * step)) + DAMPING * v1
        par = 1 - par
        vecs[3] = v2
        if last:
            send_home(2)
        forward(par, v2, gathered=False)
        rr0, mu0 = sum_last(2 * step)[0:2]
        a0 = rr0 / mu0
        r1 = r0 - a0 * v1
        u1 = v1 - a0 * v2
        lines = [fold(r1 * r1), fold(r1 * u1), fold(r1 * v1), fold(u1 * u1), fold(u1 * v1), fold(v1 * v1)]
        take(par, 2)
        par = 1 - par
        ju = y_a[1] - a0 * y_a[2]
        curve = jnp.sum(weight_a[...] * ju * ju, axis=0)
        sum_first(2 * step + 1, lines + [fold(curve)])
        if last:
            send_home(3)
        sum_second(2 * step + 1)
        rr1, ru, rv, uu, uv, vv, wuu = sum_last(2 * step + 1)[0:7]
        b1 = rr1 / rr0
        a1 = rr1 / (ru + 2.0 * b1 * rv + b1 * b1 * mu0)
        g1 = a1 * b1
        rr2 = rr1 + a1 * a1 * uu + g1 * g1 * vv - 2.0 * a1 * ru - 2.0 * g1 * rv + 2.0 * a1 * g1 * uv
        rr2 = jnp.maximum(rr2, 0.0)
        b2 = rr2 / rr1
        pr, pu, pv, p0 = 1.0 + b2, -a1, -g1, b2 * b1
        m_uu, m_uv, m_vv = wuu + 2.0 * uu, (uv - uu) / a0, (vv - uv) / a0
        curve2 = (
            pr * pr * ru + pu * pu * m_uu + pv * pv * m_vv + p0 * p0 * mu0
            + 2.0 * (pr * pu * uu + pr * pv * uv + pr * p0 * rv + pu * pv * m_uv + pu * p0 * uv + pv * p0 * vv)
        )
        a2 = rr2 / jnp.maximum(curve2, jnp.maximum(2.0 * rr2, 1e-30))
        c_r = a1 + a2 * pr
        c_u = a2 * pu
        k0 = a0 + g1 + a2 * p0 + c_r
        k1 = a2 * pv - a0 * c_r + c_u
        k2 = -a0 * c_u
        if not last:
            state = state + (k0 * r0 + k1 * v1 + k2 * v2)
            for err, y in ((err_a, y_a), (err_d, y_d)):
                err[...] = err[...] + (k0 * y[0] + k1 * y[1] + k2 * y[2])

    send_coef_a.wait_send()
    send_coef_d.wait_send()
    for n in range(4):
        sum_sent(n)
    pltpu.make_async_copy(stage_a, stage_a, init_send.at[0]).wait()
    pltpu.make_async_copy(stage_d, stage_d, init_send.at[1]).wait()
    for side, buffer in enumerate((home_a, home_d)):
        for k in range(4):
            pltpu.make_async_copy(buffer.at[k], buffer.at[k], home_sem.at[side, k]).wait()
            pltpu.make_async_copy(buffer.at[k], buffer.at[k], home_send.at[side, k]).wait()
        out[32 * side : 32 * side + 32] = buffer[0] + (k0 * buffer[1] + k1 * buffer[2] + k2 * buffer[3])


def body(coef_a, coef_d, cross_a, cross_d, time_a, time_d, height, fill):
    vmem = pl.BlockSpec(memory_space=pltpu.VMEM)
    values = pltpu.VMEM((SLOTS, 4, 128), F32)
    dma = pltpu.SemaphoreType.DMA
    out = pl.pallas_call(
        kernel,
        out_shape=jax.ShapeDtypeStruct((64, 128), F32),
        in_specs=[vmem] * 8,
        out_specs=vmem,
        scratch_shapes=[
            pltpu.VMEM((5, 64, 128), F32),
            pltpu.VMEM((16, 3, 4, 128), F32),
            pltpu.VMEM((16, 2, 4, 128), F32),
            pltpu.VMEM((SLOTS, 3, 4, 128), F32),
            pltpu.VMEM((SLOTS, 2, 4, 128), F32),
            pltpu.VMEM((2, 32, 128), F32),
            pltpu.VMEM((SLOTS, 256, 512), BF16),
            pltpu.VMEM((SLOTS, 256, 512), BF16),
            pltpu.VMEM((2, SLOTS, 2, 4, 128), F32),
            pltpu.VMEM((2, SLOTS, 2, 4, 128), F32),
            values,
            values,
            values,
            values,
            pltpu.VMEM((3, SLOTS, 4, 128), F32),
            pltpu.VMEM((3, SLOTS, 4, 128), F32),
            pltpu.VMEM((4, 64, 128), F32),
            pltpu.VMEM((4, 1, 128), F32),
            pltpu.VMEM((4, 8, 1, 128), F32),
            pltpu.VMEM((4, 1, 128), F32),
            pltpu.VMEM((4, 16, 1, 128), F32),
            pltpu.VMEM((4, 32, 128), F32),
            pltpu.VMEM((4, 32, 128), F32),
            dma((SLOTS,)),
            dma((SLOTS,)),
            dma((2,)),
            dma((2,)),
            dma((2,)),
            dma((2, SLOTS)),
            dma((2,)),
            dma((4, 2)),
            dma((4, 2)),
            dma((2, 4)),
            dma((2, 4)),
        ],
        compiler_params=pltpu.CompilerParams(collective_id=0, has_side_effects=True),
        name="adjust",
    )(coef_a, coef_d, cross_a, cross_d, time_a, time_d, height, fill.reshape(1, -1))
    return out[0:32], out[32:64]


def solution(mesh):
    rows = P(("asc", "desc"), None)
    return jax.shard_map(
        body,
        mesh=mesh,
        in_specs=(rows,) * 7 + (P(("asc", "desc")),),
        out_specs=(rows, rows),
        check_vma=False,
    )
```
